32 devices in a mesh: section: 2 (over y), tensor: 4 (over z), dp: 4 (over x, core).
Axes of the slice: x: 2, y: 2, z: 4, core: 2. Of those that a mesh axis runs over, the one named last changes fastest.
Arguments:
- tokens_in: bfloat16 [4, 256, 4, 2048], P(None, 'tensor', 'dp'), may hold values from -6 to 6
- cotangent: bfloat16 [4, 256, 4, 2048], P(None, 'tensor', 'dp'), may hold values from -6 to 6
- ln1_gain: bfloat16 [2, 2048], P('section'), may hold values from 0.5 to 1.5
- ln1_bias: bfloat16 [2, 2048], P('section'), may hold values from -1 to 1
- q_weight: bfloat16 [2, 2048, 2048], P('section', None, 'tensor'), may hold values from -0.125 to 0.125
- q_bias: bfloat16 [2, 2048], P('section', 'tensor'), may hold values from -1.5 to 1.5
- kv_weight: bfloat16 [2, 2048, 256], P('section'), may hold values from -0.125 to 0.125
- v_bias: bfloat16 [2, 128], P('section'), may hold values from -0.25 to 0.25
- o_weight: bfloat16 [2, 2048, 2048], P('section', 'tensor'), may hold values from -1.5 to 1.5
- o_bias: bfloat16 [2, 2048], P('section'), may hold values from -1.5 to 1.5
- ln2_gain: bfloat16 [2, 2048], P('section'), may hold values from 0.5 to 1.5
- ln2_bias: bfloat16 [2, 2048], P('section'), may hold values from -1 to 1
- up_weight: bfloat16 [2, 2048, 8192], P('section', None, 'tensor'), may hold values from -0.125 to 0.125
- up_bias: bfloat16 [2, 8192], P('section', 'tensor'), may hold values from -1.5 to 1.5
- down_weight: bfloat16 [2, 8192, 2048], P('section', 'tensor'), may hold values from -0.0625 to 0.0625
- down_bias: bfloat16 [2, 2048], P('section'), may hold values from -1.5 to 1.5
Outputs:
- layer_out: bfloat16 [2, 4, 256, 4, 2048], P('section', None, 'tensor', 'dp')
- input_grad: float32 [2, 4, 256, 4, 2048], P('section', None, 'tensor', 'dp')
- ln1_gain_grad: float32 [2, 2048], P('section')
- ln1_bias_grad: float32 [2, 2048], P('section')
- q_weight_grad: float32 [2, 2048, 2048], P('section', None, 'tensor')
- q_bias_grad: float32 [2, 2048], P('section', 'tensor')
- kv_weight_grad: float32 [2, 2048, 256], P('section')
- v_bias_grad: float32 [2, 128], P('section')
- o_weight_grad: float32 [2, 2048, 2048], P('section', 'tensor')
- o_bias_grad: float32 [2, 2048], P('section')
- ln2_gain_grad: float32 [2, 2048], P('section')
- ln2_bias_grad: float32 [2, 2048], P('section')
- up_weight_grad: float32 [2, 2048, 8192], P('section', None, 'tensor')
- up_bias_grad: float32 [2, 8192], P('section', 'tensor')
- down_weight_grad: float32 [2, 8192, 2048], P('section', 'tensor')
- down_bias_grad: float32 [2, 2048], P('section')
The draws below stay inside these ranges and needn't reach their ends.
All inputs are finite; a program needn't handle non-finite values.
Results may differ from the reference program's by a relative error of at most 0.022.
Values may be sent and summed in bfloat16 or wider, within the bound.
A program may use at most 512 MiB of HBM per device.

```python
import math
import jax
import jax.numpy as jnp
from jax import lax

D = 2048
HEADS = 16
HD = 128
FF = 8192
BLK = 256
NBLK = 4
SEQS = 4


def block_levels(key, shape, cuts, least, top_value):
    factor_of, own = 1.0, jax.random.fold_in(key, 6)
    for position, blocks in cuts:
        heights = jnp.exp(jax.random.uniform(jax.random.fold_in(own, position), (blocks,), jnp.float32, least / len(cuts), top_value / len(cuts)))
        factor_of = factor_of * jnp.repeat(heights, shape[position] // blocks).reshape([-1 if axis == position else 1 for axis in range(len(shape))])
    return factor_of


def gaussian(key, dims, spread, limit, cuts=(), kind=jnp.bfloat16):
    entries = spread * jax.random.normal(key, dims, jnp.float32)
    if cuts:
        entries = entries * block_levels(key, dims, cuts, -0.22, 0.18)
    return jnp.clip(entries, -limit, limit).astype(kind)


def setup_inputs(seed: int = 0) -> dict:
    key_list = jax.random.split(jax.random.key(seed), 17)
    tokens_in = gaussian(key_list[0], (NBLK, BLK, SEQS, D), 1.0, 6.0, ((1, 4), (2, 4)))
    cotangent = gaussian(key_list[1], (NBLK, BLK, SEQS, D), 1.0, 6.0, ((1, 4), (2, 4)))
    ln1_gain = jnp.clip(1.0 + 0.1 * jax.random.normal(key_list[2], (2, D), jnp.float32), 0.5, 1.5).astype(jnp.bfloat16)
    ln1_bias = gaussian(key_list[3], (2, D), 0.2, 1.0, ((0, 2),))
    q_weight = gaussian(key_list[4], (2, D, HEADS * HD), D ** -0.5, 0.125, ((0, 2), (2, 4)))
    q_bias = gaussian(key_list[5], (2, HEADS * HD), 0.3, 1.5, ((0, 2), (1, 4)))
    kv_weight = gaussian(key_list[6], (2, D, 2 * HD), D ** -0.5, 0.125, ((0, 2),))
    v_bias = gaussian(key_list[7], (2, HD), 0.05, 0.25, ((0, 2),))
    o_weight = gaussian(key_list[8], (2, HEADS * HD, D), (HEADS * HD // 128) ** -0.5, 1.5, ((0, 2), (1, 4)))
    o_bias = gaussian(key_list[9], (2, D), 0.3, 1.5, ((0, 2),))
    ln2_gain = jnp.clip(1.0 + 0.1 * jax.random.normal(key_list[10], (2, D), jnp.float32), 0.5, 1.5).astype(jnp.bfloat16)
    ln2_bias = gaussian(key_list[11], (2, D), 0.2, 1.0, ((0, 2),))
    up_weight = gaussian(key_list[12], (2, D, FF), D ** -0.5, 0.125, ((0, 2), (2, 4)))
    up_bias = gaussian(key_list[13], (2, FF), 0.3, 1.5, ((0, 2), (1, 4)))
    down_weight = gaussian(key_list[14], (2, FF, D), FF ** -0.5, 0.0625, ((0, 2), (1, 4)))
    down_bias = gaussian(key_list[15], (2, D), 0.3, 1.5, ((0, 2),))
    return {"tokens_in": tokens_in, "cotangent": cotangent, "ln1_gain": ln1_gain, "ln1_bias": ln1_bias, "q_weight": q_weight, "q_bias": q_bias, "kv_weight": kv_weight, "v_bias": v_bias, "o_weight": o_weight, "o_bias": o_bias, "ln2_gain": ln2_gain, "ln2_bias": ln2_bias, "up_weight": up_weight, "up_bias": up_bias, "down_weight": down_weight, "down_bias": down_bias}


HIGH = lax.Precision.HIGHEST

@jax.custom_vjp
def low(v):
    return lax.optimization_barrier(v.astype(jnp.bfloat16)).astype(jnp.float32)

@jax.custom_vjp
def low_back(v):
    return v

def low_keep(v):
    return (low(v), None)

def low_pass(kept, grad):
    return (grad,)

def back_keep(v):
    return (v, None)

def back_low(kept, grad):
    return (low(grad),)
low.defvjp(low_keep, low_pass)
low_back.defvjp(back_keep, back_low)

def layer_norm(values, gain_vec, bias_vec):
    row_mean = lax.optimization_barrier(jnp.mean(values, axis=-1, keepdims=True))
    centred = values - row_mean
    row_var = lax.optimization_barrier(jnp.mean(centred * centred, axis=-1, keepdims=True))
    return centred * lax.rsqrt(row_var + 1e-05) * gain_vec + bias_vec

def one_layer(layer_input, params):
    gain_one, bias_one, w_query, b_query, w_pairs, b_value, w_out, b_out, gain_two, bias_two, w_up, b_up, w_down, b_down = params
    groups = layer_input.shape[0]
    normed = low(layer_norm(layer_input, gain_one, bias_one))
    queries = low_back(low(jnp.matmul(normed, w_query, precision=HIGH) + b_query))
    pair_bias = jnp.concatenate([jnp.zeros((HD,), jnp.float32), b_value])
    pairs = low_back(low(jnp.matmul(normed, w_pairs, precision=HIGH) + pair_bias))
    key_rows = pairs[..., :HD]
    value_rows = pairs[..., HD:]
    per_block = queries.reshape(groups, NBLK, BLK, HEADS, HD).transpose(1, 0, 2, 3, 4)
    score_scale = 1.0 / math.sqrt(HD)
    positions = jnp.arange(NBLK * BLK, dtype=jnp.int32)

    def attend(block_item):
        block_query, block_index = block_item
        scores = jnp.einsum('gqhd,gkd->gqhk', block_query, key_rows, precision=HIGH) * score_scale
        visible = positions < (block_index + 1) * BLK
        scores = low_back(jnp.where(visible, scores, -1e+30))
        row_top = lax.optimization_barrier(jnp.max(scores, axis=-1, keepdims=True))
        exponent = jnp.exp(scores - row_top)
        probabilities = low(exponent / lax.optimization_barrier(jnp.sum(exponent, axis=-1, keepdims=True)))
        return jnp.einsum('gqhk,gkd->gqhd', probabilities, value_rows, precision=HIGH)
    attended = lax.map(jax.checkpoint(attend), (per_block, jnp.arange(NBLK, dtype=jnp.int32)))
    attended = attended.transpose(1, 0, 2, 3, 4).reshape(groups, NBLK * BLK, HEADS * HD)
    attended = low_back(low(attended))
    hidden = layer_input + low_back(jnp.matmul(attended, w_out, precision=HIGH)) + b_out
    normed_two = low(layer_norm(hidden, gain_two, bias_two))
    pre_active = low_back(jnp.matmul(normed_two, w_up, precision=HIGH) + b_up)
    active = low(jax.nn.gelu(pre_active, approximate=True))
    return hidden + low_back(jnp.matmul(active, w_down, precision=HIGH)) + b_down

def rounded_layer(layer_input, params):
    return low(one_layer(layer_input, params))

def reference(tokens_in, cotangent, ln1_gain, ln1_bias, q_weight, q_bias, kv_weight, v_bias, o_weight, o_bias, ln2_gain, ln2_bias, up_weight, up_bias, down_weight, down_bias):
    weights = (ln1_gain, ln1_bias, q_weight, q_bias, kv_weight, v_bias, o_weight, o_bias, ln2_gain, ln2_bias, up_weight, up_bias, down_weight, down_bias)
    first_layer = tuple((weight[0].astype(jnp.float32) for weight in weights))
    second_layer = tuple((weight[1].astype(jnp.float32) for weight in weights))
    sequences = tokens_in.shape[2]
    group_size = math.gcd(sequences, 4)
    length = NBLK * BLK

    def arrange(array):
        whole = array.astype(jnp.float32).transpose(2, 0, 1, 3).reshape(sequences, length, D)
        return whole.reshape(sequences // group_size, group_size, length, D)

    def restore(array):
        return array.reshape(sequences, NBLK, BLK, D).transpose(1, 2, 0, 3)

    def group_step(totals, group_item):
        inputs, grad_final = group_item
        middle, back_first = jax.vjp(rounded_layer, inputs, first_layer)
        final, back_second = jax.vjp(rounded_layer, middle, second_layer)
        grad_middle, grads_second = back_second(grad_final)
        grad_inputs, grads_first = back_first(grad_middle)
        totals = (jax.tree.map(jnp.add, totals[0], grads_first), jax.tree.map(jnp.add, totals[1], grads_second))
        return (totals, (middle, final, grad_inputs, grad_middle))
    start = (jax.tree.map(jnp.zeros_like, first_layer), jax.tree.map(jnp.zeros_like, second_layer))
    totals, results = lax.scan(group_step, start, (arrange(tokens_in), arrange(cotangent)))
    middle, final, grad_inputs, grad_middle = results
    layer_out = jnp.stack([restore(middle), restore(final)]).astype(jnp.bfloat16)
    input_grad = jnp.stack([restore(grad_inputs), restore(grad_middle)])
    grads = tuple((jnp.stack([first_grad, second_grad]) for first_grad, second_grad in zip(totals[0], totals[1])))
    return (layer_out, input_grad, grads[0], grads[1], grads[2], grads[3], grads[4], grads[5], grads[6], grads[7], grads[8], grads[9], grads[10], grads[11], grads[12], grads[13])
```

```python
import math

import jax
import jax.numpy as jnp
from jax import lax
from jax.sharding import PartitionSpec as P

HD = 128
F32 = jnp.float32
BF16 = jnp.bfloat16


def from_behind(block, axis, distance):
    devices = range(lax.axis_size(axis))
    route = [(i - distance, i) for i in devices if i - distance in devices]
    return lax.ppermute(block, axis, route)


def layer_norm(values, gain_vec, bias_vec):
    row_mean = jnp.mean(values, axis=-1, keepdims=True)
    centred = values - row_mean
    row_var = jnp.mean(centred * centred, axis=-1, keepdims=True)
    return centred * lax.rsqrt(row_var + 1e-05) * gain_vec + bias_vec


def gelu_tanh(values):
    return jax.nn.gelu(values, approximate=True)


def dot(a, b):
    return jnp.dot(a, b, preferred_element_type=F32)


def dot_t(a, b):
    return lax.dot_general(a, b, (((1,), (1,)), ((), ())), preferred_element_type=F32)


def t_dot(a, b):
    return lax.dot_general(a, b, (((0,), (0,)), ((), ())), preferred_element_type=F32)


def gather_rows(own_rows):
    return lax.all_gather(own_rows, "tensor", axis=0, tiled=True)


def sum_rows(partial):
    return lax.psum_scatter(
        partial.astype(BF16), "tensor", scatter_dimension=0, tiled=True
    ).astype(F32)


def swap(value, distance):
    size = lax.axis_size("dp")
    return lax.ppermute(value, "dp", [(i, i ^ distance) for i in range(size)])


def fold(value, distance, axis):
    bit = (lax.axis_index("dp") // distance) % 2
    half = value.shape[axis] // 2
    away = lax.dynamic_slice_in_dim(value, (1 - bit) * half, half, axis)
    kept = lax.dynamic_slice_in_dim(value, bit * half, half, axis)
    return kept + swap(away.astype(BF16), distance).astype(F32)


def unfold(value, distance, axis):
    bit = (lax.axis_index("dp") // distance) % 2
    other = swap(value, distance)
    low = jnp.where(bit == 0, value, other)
    high = jnp.where(bit == 0, other, value)
    return jnp.concatenate([low, high], axis=axis)


def sum_dp(value, axis, scatter=None):
    size = lax.axis_size("dp")
    distance = 1
    while distance < size:
        value = fold(value, distance, axis)
        if distance == 1 and scatter is not None:
            value = lax.psum_scatter(
                value.astype(BF16), "tensor", scatter_dimension=scatter, tiled=True
            ).astype(F32)
        distance *= 2
    value = value.astype(BF16)
    while distance > 1:
        distance //= 2
        value = unfold(value, distance, axis)
    return value.astype(F32)


def whole_weight(shard, split, join):
    size = lax.axis_size("dp")
    part = shard.shape[split] // size
    own = lax.dynamic_slice_in_dim(shard, lax.axis_index("dp") * part, part, split)
    own = lax.all_gather(own, "tensor", axis=join, tiled=True)
    return lax.all_gather(own, "dp", axis=split, tiled=True)


def on_device(
    tokens_in,
    cotangent,
    ln1_gain,
    ln1_bias,
    q_weight,
    q_bias,
    kv_weight,
    v_bias,
    o_weight,
    o_bias,
    ln2_gain,
    ln2_bias,
    up_weight,
    up_bias,
    down_weight,
    down_bias,
):
    section = lax.axis_index("section")
    tensor_count = lax.axis_size("tensor")
    tensor_rank = lax.axis_index("tensor")
    gain_one = ln1_gain[0].astype(F32)
    bias_one = ln1_bias[0].astype(F32)
    w_pairs = kv_weight[0]
    pair_bias = jnp.concatenate([jnp.zeros((HD,), F32), v_bias[0].astype(F32)])
    b_out = o_bias[0].astype(F32)
    gain_two = ln2_gain[0].astype(F32)
    bias_two = ln2_bias[0].astype(F32)
    w_up = up_weight[0]
    b_up = up_bias[0].astype(F32)
    w_down = down_weight[0]
    b_down = down_bias[0].astype(F32)
    blocks, own_count, seq_count, model_dim = tokens_in.shape
    assert seq_count == 1
    tokens_in = tokens_in[:, :, 0]
    cotangent = cotangent[:, :, 0]
    block_len = own_count * tensor_count
    total_len = blocks * block_len
    w_query = whole_weight(q_weight[0], 0, 1)
    w_out = whole_weight(o_weight[0], 1, 0)
    b_query = lax.all_gather(q_bias[0], "tensor", axis=0, tiled=True).astype(F32)
    heads = w_query.shape[1] // HD
    width = heads * HD
    ff_local = w_up.shape[1]
    score_scale = 1.0 / math.sqrt(HD)
    positions = jnp.arange(total_len, dtype=jnp.int32)

    def zeros(shape, dtype):
        return jnp.zeros(shape, dtype)

    kept_normed = zeros((blocks, own_count, model_dim), BF16)
    kept_query = zeros((blocks, own_count, width), BF16)
    kept_attended = zeros((blocks, own_count, width), BF16)
    kept_logsum = zeros((blocks, own_count * heads), F32)
    kv_cache = zeros((total_len, 2 * HD), BF16)
    kept_input = zeros((blocks, own_count, model_dim), F32)
    kept_hidden = zeros((blocks, own_count, model_dim), F32)
    kept_normed_two = zeros((blocks, block_len, model_dim), BF16)
    kept_pre = zeros((blocks, block_len, ff_local), F32)
    kept_active = zeros((blocks, block_len, ff_local), BF16)
    outputs = zeros((blocks, own_count, model_dim), BF16)
    received = zeros((own_count, model_dim), F32)

    def put(kept, value, index):
        return lax.dynamic_update_index_in_dim(kept, value, index, 0)

    def take(kept, index):
        return lax.dynamic_index_in_dim(kept, index, 0, keepdims=False)

    for turn in range(blocks + 1):
        block_index = jnp.clip(turn - section, 0, blocks - 1)
        layer_input = jnp.where(section == 0, take(tokens_in, block_index).astype(F32), received)
        normed = layer_norm(layer_input, gain_one, bias_one).astype(BF16)
        pairs = gather_rows((dot(normed, w_pairs) + pair_bias).astype(BF16))
        kv_cache = lax.dynamic_update_slice_in_dim(kv_cache, pairs, block_index * block_len, 0)
        query = (dot(normed, w_query) + b_query).astype(BF16)
        visible = positions < (block_index + 1) * block_len
        query_rows = query.reshape(own_count * heads, HD)
        scores = dot_t(query_rows, kv_cache[:, :HD]) * score_scale
        scores = jnp.where(visible, scores, -1e30)
        row_top = jnp.max(scores, axis=-1, keepdims=True)
        exponent = jnp.exp(scores - row_top)
        row_total = jnp.sum(exponent, axis=-1, keepdims=True)
        log_total = (row_top + jnp.log(row_total))[:, 0]
        weights_low = (exponent / row_total).astype(BF16)
        attended = dot(weights_low, kv_cache[:, HD:]).astype(BF16).reshape(own_count, width)
        hidden = layer_input + dot(attended, w_out) + b_out
        normed_two = gather_rows(layer_norm(hidden, gain_two, bias_two).astype(BF16))
        pre_active = dot(normed_two, w_up) + b_up
        active = gelu_tanh(pre_active).astype(BF16)
        result_low = (hidden + sum_rows(dot(active, w_down)) + b_down).astype(BF16)
        kept_normed = put(kept_normed, normed, block_index)
        kept_query = put(kept_query, query, block_index)
        kept_attended = put(kept_attended, attended, block_index)
        kept_logsum = put(kept_logsum, log_total, block_index)
        kept_input = put(kept_input, layer_input, block_index)
        kept_hidden = put(kept_hidden, hidden, block_index)
        kept_normed_two = put(kept_normed_two, normed_two, block_index)
        kept_pre = put(kept_pre, pre_active, block_index)
        kept_active = put(kept_active, active, block_index)
        outputs = put(outputs, result_low, block_index)
        if turn < blocks:
            received = from_behind(result_low, "section", 1).astype(F32)

    key_rows = kv_cache[:, :HD]
    value_rows = kv_cache[:, HD:]
    kept_grad_mlp = zeros((blocks + 1, block_len, model_dim), BF16)
    kept_grad_pre = zeros((blocks + 1, block_len, ff_local), BF16)
    kept_branch = zeros((blocks + 1, own_count, model_dim), BF16)
    kept_grad_query = zeros((blocks + 1, own_count, width), BF16)
    kept_grad_pairs = zeros((blocks + 1, own_count, 2 * HD), BF16)
    input_grads = zeros((blocks + 1, own_count, model_dim), F32)
    pair_grad_acc = zeros((total_len, 2 * HD), F32)
    received_back = zeros((own_count, model_dim), F32)
    common = [zeros((model_dim,), F32) for _ in range(6)]
    for turn in range(blocks + 1):
        step_count = turn - (1 - section)
        valid = (step_count >= 0) & (step_count < blocks)
        block_index = blocks - 1 - jnp.clip(step_count, 0, blocks - 1)
        slot = jnp.where(valid, block_index, blocks)
        grad_out = jnp.where(section == 1, take(cotangent, block_index).astype(F32), received_back)
        grad_out = grad_out * valid.astype(F32)
        pre_active = take(kept_pre, block_index)
        grad_mlp = gather_rows(grad_out.astype(BF16))
        grad_active = dot_t(grad_mlp, w_down)
        grad_pre = jax.vjp(gelu_tanh, pre_active)[1](grad_active)[0].astype(BF16)
        grad_normed_two = sum_rows(dot_t(grad_pre, w_up))
        norm_back_two = jax.vjp(layer_norm, take(kept_hidden, block_index), gain_two, bias_two)[1]
        grad_hidden_norm, gain_two_term, bias_two_term = norm_back_two(grad_normed_two)
        grad_hidden = grad_out + grad_hidden_norm
        branch = grad_hidden.astype(BF16)
        grad_attended = dot_t(branch, w_out).astype(BF16).reshape(own_count * heads, HD)
        query_rows = take(kept_query, block_index).reshape(own_count * heads, HD)
        log_total = take(kept_logsum, block_index)
        visible = positions < (block_index + 1) * block_len
        scores = dot_t(query_rows, key_rows) * score_scale
        scores = jnp.where(visible, scores, -1e30)
        probabilities = jnp.exp(scores - log_total[:, None])
        grad_probs = dot_t(grad_attended, value_rows)
        row_inner = jnp.sum(probabilities * grad_probs, axis=-1, keepdims=True)
        grad_scores = (probabilities * (grad_probs - row_inner)).astype(BF16)
        grad_query = (dot(grad_scores, key_rows) * score_scale).astype(BF16)
        grad_query = grad_query.reshape(own_count, width)
        grad_keys = t_dot(grad_scores, query_rows) * score_scale
        grad_values = t_dot(probabilities.astype(BF16), grad_attended)
        pair_grad_acc = pair_grad_acc + jnp.concatenate([grad_keys, grad_values], axis=-1)
        block_pairs = lax.dynamic_slice_in_dim(pair_grad_acc, block_index * block_len, block_len, 0)
        grad_pairs = sum_rows(block_pairs).astype(BF16)
        grad_normed = dot_t(grad_query, w_query) + dot_t(grad_pairs, w_pairs)
        norm_back_one = jax.vjp(layer_norm, take(kept_input, block_index), gain_one, bias_one)[1]
        grad_input_norm, gain_one_term, bias_one_term = norm_back_one(grad_normed)
        grad_input = grad_hidden + grad_input_norm
        if turn < blocks:
            received_back = from_behind(grad_input.astype(BF16), "section", -1).astype(F32)
        scale = valid.astype(F32)
        terms = (
            gain_one_term * scale,
            bias_one_term * scale,
            jnp.sum(grad_hidden, axis=0),
            gain_two_term,
            bias_two_term,
            jnp.sum(grad_out, axis=0),
        )
        common = [total + term for total, term in zip(common, terms)]
        input_grads = put(input_grads, grad_input, slot)
        kept_grad_mlp = put(kept_grad_mlp, grad_mlp, slot)
        kept_grad_pre = put(kept_grad_pre, grad_pre, slot)
        kept_branch = put(kept_branch, branch, slot)
        kept_grad_query = put(kept_grad_query, grad_query, slot)
        kept_grad_pairs = put(kept_grad_pairs, grad_pairs, slot)

    def flat(kept):
        return kept[:blocks].reshape(-1, kept.shape[-1])

    down_w = t_dot(flat(kept_active), flat(kept_grad_mlp))
    up_w = t_dot(flat(kept_normed_two), flat(kept_grad_pre))
    up_b = jnp.sum(flat(kept_grad_pre).astype(F32), axis=0)
    out_w = t_dot(flat(kept_attended), flat(kept_branch))
    query_w = t_dot(flat(kept_normed), flat(kept_grad_query))
    query_b = jnp.sum(flat(kept_grad_query).astype(F32), axis=0)
    pair_w = t_dot(flat(kept_normed), flat(kept_grad_pairs))
    value_b = jnp.sum(flat(kept_grad_pairs)[:, HD:].astype(F32), axis=0)
    down_w = sum_dp(down_w, 0)
    up_w = sum_dp(up_w, 0)
    out_w = sum_dp(out_w, 1, 0)
    query_w = sum_dp(query_w, 0, 1)
    pair_w = lax.psum(pair_w.astype(BF16), ("tensor", "dp")).astype(F32)
    wide = jnp.zeros((tensor_count, ff_local), F32)
    wide = lax.dynamic_update_index_in_dim(wide, up_b, tensor_rank, 0)
    packed = jnp.concatenate([*common, query_b, value_b, wide.reshape(-1)])
    packed = lax.psum(packed, ("tensor", "dp"))
    vecs = packed[: 6 * model_dim].reshape(6, model_dim)
    own_query = lax.dynamic_slice_in_dim(
        packed, 6 * model_dim + tensor_rank * (width // tensor_count), width // tensor_count, 0
    )
    value_b = lax.slice_in_dim(packed, 6 * model_dim + width, 6 * model_dim + width + HD)
    own_up = lax.dynamic_slice_in_dim(
        packed, 6 * model_dim + width + HD + tensor_rank * ff_local, ff_local, 0
    )
    return (
        outputs[None, :, :, None],
        input_grads[None, :blocks, :, None],
        vecs[0][None],
        vecs[1][None],
        query_w[None],
        own_query[None],
        pair_w[None],
        value_b[None],
        out_w[None],
        vecs[2][None],
        vecs[3][None],
        vecs[4][None],
        up_w[None],
        own_up[None],
        down_w[None],
        vecs[5][None],
    )


def solution(mesh):
    placed = (
        P(None, "tensor", "dp", None),
        P(None, "tensor", "dp", None),
        P("section", None),
        P("section", None),
        P("section", None, "tensor"),
        P("section", "tensor"),
        P("section", None, None),
        P("section", None),
        P("section", "tensor", None),
        P("section", None),
        P("section", None),
        P("section", None),
        P("section", None, "tensor"),
        P("section", "tensor"),
        P("section", "tensor", None),
        P("section", None),
    )
    return jax.shard_map(
        on_device,
        mesh=mesh,
        in_specs=placed,
        out_specs=(
            P("section", None, "tensor", "dp", None),
            P("section", None, "tensor", "dp", None),
            P("section", None),
            P("section", None),
            P("section", None, "tensor"),
            P("section", "tensor"),
            P("section", None, None),
            P("section", None),
            P("section", "tensor", None),
            P("section", None),
            P("section", None),
            P("section", None),
            P("section", None, "tensor"),
            P("section", "tensor"),
            P("section", "tensor", None),
            P("section", None),
        ),
        check_vma=False,
    )
```

```python
import functools
import math

import jax
import jax.numpy as jnp
from jax import lax
from jax.experimental import pallas as pl
from jax.experimental.pallas import tpu as pltpu
from jax.sharding import PartitionSpec as P

HD = 128
F32 = jnp.float32
BF16 = jnp.bfloat16
MESH = pl.DeviceIdType.MESH
GELU_A = math.sqrt(2.0 / math.pi)
GELU_B = 0.044715


def dot(a, b):
    return jnp.dot(a, b, preferred_element_type=F32)


def dot_t(a, b):
    return lax.dot_general(a, b, (((1,), (1,)), ((), ())), preferred_element_type=F32)


def aligned(start, size):
    return pl.ds(pl.multiple_of(start, size), size)


def greet(n):
    me = lax.axis_index("tensor")
    barrier = pltpu.get_barrier_semaphore()
    for k in range(1, n):
        pl.semaphore_signal(
            barrier, inc=1, device_id={"tensor": lax.rem(me + k, n)}, device_id_type=MESH
        )
    pl.semaphore_signal(
        barrier, inc=1, device_id={"section": 1 - lax.axis_index("section")}, device_id_type=MESH
    )
    pl.semaphore_wait(barrier, n)


def normalize(v):
    mean = jnp.mean(v, axis=-1, keepdims=True)
    centred = v - mean
    var = jnp.mean(centred * centred, axis=-1, keepdims=True)
    rstd = lax.rsqrt(var + 1e-05)
    return centred * rstd, rstd


def line_rounds(n, chunks, rows, bufs, compute, finish):
    (g, terms, sum_r, sum_l, in_l, in_r) = bufs["refs"]
    (gs_r, gs_l, g_recv, rs_r, rs_l, rr_l, rr_r) = bufs["sems"]
    me = lax.axis_index("tensor")

    def part(j):
        return pl.ds(pl.multiple_of(j * rows, rows), rows)

    def gather_copy(c, j, step, to_right):
        return pltpu.make_async_remote_copy(
            src_ref=g.at[c, part(j)],
            dst_ref=g.at[c, part(j)],
            send_sem=(gs_r if to_right else gs_l).at[c, step],
            recv_sem=g_recv.at[c, j],
            device_id={"tensor": jnp.minimum(me + 1, n - 1) if to_right else jnp.maximum(me - 1, 0)},
            device_id_type=MESH,
        )

    def sum_copy(c, j, to_right):
        return pltpu.make_async_remote_copy(
            src_ref=(sum_r if to_right else sum_l).at[c, part(j)],
            dst_ref=(in_l if to_right else in_r).at[c, part(j)],
            send_sem=(rs_r if to_right else rs_l).at[c, j],
            recv_sem=(rr_l if to_right else rr_r).at[c, j],
            device_id={"tensor": jnp.minimum(me + 1, n - 1) if to_right else jnp.maximum(me - 1, 0)},
            device_id_type=MESH,
        )

    def slot(s, carry):
        for h in range(n):
            c = s - h

            @pl.when((c >= 0) & (c < chunks))
            def _(h=h, c=c):
                from_l = me - h >= 0
                from_r = me + h <= n - 1
                if h > 0:

                    @pl.when(from_l)
                    def _():
                        gather_copy(c, jnp.maximum(me - h, 0), 0, True).wait_recv()

                    @pl.when(from_r)
                    def _():
                        gather_copy(c, jnp.minimum(me + h, n - 1), 0, False).wait_recv()

                if h < n - 1:

                    @pl.when(from_l & (me < n - 1))
                    def _():
                        gather_copy(c, jnp.maximum(me - h, 0), h, True).start()

                    @pl.when(from_r & (me > 0))
                    def _():
                        gather_copy(c, jnp.minimum(me + h, n - 1), h, False).start()

        for h in range(n - 1):
            c = s - n - h

            @pl.when((c >= 0) & (c < chunks))
            def _(h=h, c=c):
                if h == 0:
                    finish(c, "kept")

                @pl.when((h >= me) & (me < n - 1))
                def _():
                    j = jnp.minimum(n - 1 - (h - me), n - 1)

                    @pl.when(me > 0)
                    def _():
                        sum_copy(c, j, True).wait_recv()
                        sum_r[c, part(j)] = (terms[c, part(j)] + in_l[c, part(j)].astype(F32)).astype(BF16)

                    @pl.when(me == 0)
                    def _():
                        sum_r[c, part(j)] = terms[c, part(j)].astype(BF16)

                    sum_copy(c, j, True).start()

                @pl.when((h >= n - 1 - me) & (me > 0))
                def _():
                    j = jnp.maximum(h - (n - 1 - me), 0)

                    @pl.when(me < n - 1)
                    def _():
                        sum_copy(c, j, False).wait_recv()
                        sum_l[c, part(j)] = (terms[c, part(j)] + in_r[c, part(j)].astype(F32)).astype(BF16)

                    @pl.when(me == n - 1)
                    def _():
                        sum_l[c, part(j)] = terms[c, part(j)].astype(BF16)

                    sum_copy(c, j, False).start()

        c_done = s - (2 * n - 1)

        @pl.when((c_done >= 0) & (c_done < chunks))
        def _():
            @pl.when(me > 0)
            def _():
                sum_copy(c_done, me, True).wait_recv()
                terms[c_done, part(me)] += in_l[c_done, part(me)].astype(F32)

            @pl.when(me < n - 1)
            def _():
                sum_copy(c_done, me, False).wait_recv()
                terms[c_done, part(me)] += in_r[c_done, part(me)].astype(F32)

        c_now = s - (n - 1)

        @pl.when((c_now >= 0) & (c_now < chunks))
        def _():
            compute(c_now)

        return carry

    lax.fori_loop(0, chunks + 2 * n - 1, slot, 0)

    def drain(c, carry):
        for h in range(n - 1):

            @pl.when((me - h >= 0) & (me < n - 1))
            def _(h=h):
                gather_copy(c, jnp.maximum(me - h, 0), h, True).wait_send()

            @pl.when((me + h <= n - 1) & (me > 0))
            def _(h=h):
                gather_copy(c, jnp.minimum(me + h, n - 1), h, False).wait_send()

        for j in range(n):

            @pl.when(j > me)
            def _(j=j):
                sum_copy(c, j, True).wait_send()

            @pl.when(j < me)
            def _(j=j):
                sum_copy(c, j, False).wait_send()

        return carry

    lax.fori_loop(0, chunks, drain, 0)


def line_scratch(n, chunks, rows, width):
    whole = n * rows
    refs = [
        pltpu.VMEM((chunks, whole, width), BF16),
        pltpu.VMEM((chunks, whole, width), F32),
    ] + [pltpu.VMEM((chunks, whole, width), BF16)] * 4
    sems = [pltpu.SemaphoreType.DMA((chunks, n))] * 7
    return refs, sems


def forward_kernel(
    cfg,
    tokens,
    w_q_hbm,
    w_o_hbm,
    w_up_hbm,
    w_dn_hbm,
    w_kv,
    vecs,
    up_bias,
    pair_bias,
    normed_out,
    query_out,
    att_out,
    lse_out,
    input_out,
    hidden_out,
    result_out,
    kv_out,
    two_hbm,
    act_hbm,
    slope_hbm,
    w_q,
    w_o,
    w_up,
    w_dn,
    x_ref,
    q_ref,
    v_t,
    s_ref,
    act,
    slope,
    inbox,
    g,
    terms,
    sum_r,
    sum_l,
    in_l,
    in_r,
    gs_r,
    gs_l,
    g_recv,
    rs_r,
    rs_l,
    rr_l,
    rr_r,
    w_sem,
    kv_send,
    kv_recv,
    keep_sem,
    hand_send,
    hand_recv,
):
    n, nb, own, chunks, rows, tile = (cfg[k] for k in ("n", "nb", "own", "chunks", "rows", "tile"))
    dim = x_ref.shape[1]
    ff = w_up.shape[1]
    width = w_q.shape[1]
    heads = width // HD
    block = n * own
    per = cfg["per"]
    me = lax.axis_index("tensor")
    sec = lax.axis_index("section")
    scale = 1.0 / math.sqrt(HD)
    loads = [
        pltpu.make_async_copy(src, dst, w_sem.at[k])
        for k, (src, dst) in enumerate(((w_q_hbm, w_q), (w_o_hbm, w_o), (w_up_hbm, w_up), (w_dn_hbm, w_dn)))
    ]
    for load in loads:
        load.start()
    greet(n)

    def pairs_copy(b, k):
        rows_here = aligned(b * block + me * own, own)
        return pltpu.make_async_remote_copy(
            src_ref=kv_out.at[rows_here],
            dst_ref=kv_out.at[rows_here],
            send_sem=kv_send.at[k],
            recv_sem=kv_recv.at[k],
            device_id={"tensor": lax.rem(me + k, n)},
            device_id_type=MESH,
        )

    def hand_copy(b):
        return pltpu.make_async_remote_copy(
            src_ref=result_out.at[b],
            dst_ref=inbox.at[b],
            send_sem=hand_send.at[b],
            recv_sem=hand_recv.at[b],
            device_id={"section": 1 - sec},
            device_id_type=MESH,
        )

    def keep_copies(b, c):
        return [
            pltpu.make_async_copy(g.at[c], two_hbm.at[b, c], keep_sem.at[0, c]),
            pltpu.make_async_copy(act.at[c], act_hbm.at[b, c], keep_sem.at[1, c]),
            pltpu.make_async_copy(slope.at[c], slope_hbm.at[b, c], keep_sem.at[2, c]),
        ]

    def block_step(b, carry):
        @pl.when(sec == 0)
        def _():
            input_out[b] = tokens[b]

        @pl.when(sec != 0)
        def _():
            hand_copy(b).wait_recv()
            input_out[b] = inbox[b]

        x_ref[...] = input_out[b].astype(F32)
        unit, _ = normalize(x_ref[...])
        normed = (unit * vecs[0:1] + vecs[1:2]).astype(BF16)
        normed_out[b] = normed
        pairs = (dot(normed, w_kv[...]) + pair_bias[...]).astype(BF16)
        kv_out[aligned(b * block + me * own, own)] = pairs
        for k in range(1, n):
            pairs_copy(b, k).start()

        @pl.when(b == 0)
        def _():
            loads[0].wait()

        def query_tile(t, carry):
            cols = aligned(t * tile, tile)
            q = (dot(normed_out[b], w_q[:, cols]) + vecs[6:7, cols]).astype(BF16)
            for k in range(tile // HD):
                q_ref[aligned((t * (tile // HD) + k) * own, own)] = q[:, k * HD : (k + 1) * HD]
            return carry

        lax.fori_loop(0, width // tile, query_tile, 0)
        query_out[b] = q_ref[...]
        for k in range(1, n):
            pairs_copy(b, k).wait_recv()
        here = aligned(b * block, block)
        v_t[b] = kv_out[here, HD:].astype(F32).T.astype(BF16)

        def head_tile(t, carry):
            q = q_ref[aligned(t * per * own, per * own)]

            def score(kb, top):
                s = dot_t(kv_out[aligned(kb * block, block), :HD], q) * scale
                s_ref[kb] = s
                return jnp.maximum(top, jnp.max(s, axis=0, keepdims=True))

            top = lax.fori_loop(0, b + 1, score, jnp.full((1, per * own), -jnp.inf, F32))

            def weigh(kb, state):
                total, acc = state
                e = jnp.exp(s_ref[kb] - top)
                return total + jnp.sum(e, axis=0, keepdims=True), acc + dot(v_t[kb], e.astype(BF16))

            total, acc = lax.fori_loop(
                0,
                b + 1,
                weigh,
                (jnp.zeros((1, per * own), F32), jnp.zeros((HD, per * own), F32)),
            )
            lse_out[b, t] = top + jnp.log(total)
            mixed = (acc / total).T.astype(BF16)
            for k in range(per):
                att_out[b, :, aligned((t * per + k) * HD, HD)] = mixed[k * own : (k + 1) * own]
            return carry

        lax.fori_loop(0, heads // per, head_tile, 0)

        @pl.when(b == 0)
        def _():
            loads[1].wait()

        def out_tile(t, carry):
            cols = aligned(t * tile, tile)
            hidden_out[b, :, cols] = (
                x_ref[:, cols] + dot(att_out[b], w_o[:, cols]) + vecs[4:5, cols]
            )
            return carry

        lax.fori_loop(0, dim // tile, out_tile, 0)
        unit, _ = normalize(hidden_out[b])
        normed_two = (unit * vecs[2:3] + vecs[3:4]).astype(BF16)
        for c in range(chunks):
            g[c, aligned(me * rows, rows)] = normed_two[c * rows : (c + 1) * rows]

        @pl.when(b == 0)
        def _():
            loads[2].wait()
            loads[3].wait()

        def compute(c):
            def up_tile(t, carry):
                cols = aligned(t * tile, tile)
                pre = dot(g[c], w_up[:, cols]) + up_bias[:, cols]
                inner = GELU_A * (pre + GELU_B * pre * pre * pre)
                th = jnp.tanh(inner)
                half = 0.5 * (1.0 + th)
                act[c, :, cols] = (pre * half).astype(BF16)
                slope[c, :, cols] = (
                    half + 0.5 * pre * (1.0 - th * th) * (GELU_A * (1.0 + 3.0 * GELU_B * pre * pre))
                ).astype(BF16)
                return carry

            lax.fori_loop(0, ff // tile, up_tile, 0)

            def down_tile(t, carry):
                cols = aligned(t * tile, tile)
                terms[c, :, cols] = dot(act[c], w_dn[:, cols])
                return carry

            lax.fori_loop(0, dim // tile, down_tile, 0)
            for copy in keep_copies(b, c):
                copy.start()

        def finish(c, what):
            for copy in keep_copies(b, c):
                copy.wait()

        line_rounds(
            n,
            chunks,
            rows,
            {
                "refs": (g, terms, sum_r, sum_l, in_l, in_r),
                "sems": (gs_r, gs_l, g_recv, rs_r, rs_l, rr_l, rr_r),
            },
            compute,
            finish,
        )
        for c in range(chunks):
            part = slice(c * rows, (c + 1) * rows)
            result_out[b, part] = (
                hidden_out[b, part] + terms[c, aligned(me * rows, rows)] + vecs[5:6]
            ).astype(BF16)

        @pl.when(sec == 0)
        def _():
            hand_copy(b).start()

        for k in range(1, n):
            pairs_copy(b, k).wait_send()
        return carry

    lax.fori_loop(0, nb, block_step, 0)

    def settle(b, carry):
        @pl.when(sec == 0)
        def _():
            hand_copy(b).wait_send()

        return carry

    lax.fori_loop(0, nb, settle, 0)


def forward(tokens, w_q, w_o, w_up, w_dn, w_kv, vecs, up_bias, pair_bias):
    n = lax.axis_size("tensor")
    nb, own, dim = tokens.shape
    rows = min(16, own)
    chunks = own // rows
    ff = w_up.shape[1]
    width = w_q.shape[1]
    heads = width // HD
    tile = min(512, dim, ff)
    per = min(heads, max(1, 256 // own))
    block = n * own
    cfg = dict(n=n, nb=nb, own=own, chunks=chunks, rows=rows, tile=tile, per=per)
    S = jax.ShapeDtypeStruct
    vmem = pl.BlockSpec(memory_space=pltpu.VMEM)
    hbm = pl.BlockSpec(memory_space=pl.ANY)
    line_refs, line_sems = line_scratch(n, chunks, rows, dim)
    dma = pltpu.SemaphoreType.DMA
    return pl.pallas_call(
        functools.partial(forward_kernel, cfg),
        name="forward",
        out_shape=(
            S((nb, own, dim), BF16),
            S((nb, heads * own, HD), BF16),
            S((nb, own, width), BF16),
            S((nb, heads // per, 1, per * own), F32),
            S((nb, own, dim), BF16),
            S((nb, own, dim), F32),
            S((nb, own, dim), BF16),
            S((nb * block, 2 * HD), BF16),
            S((nb, chunks, n * rows, dim), BF16),
            S((nb, chunks, n * rows, ff), BF16),
            S((nb, chunks, n * rows, ff), BF16),
        ),
        in_specs=[vmem, hbm, hbm, hbm, hbm, vmem, vmem, vmem, vmem],
        out_specs=(vmem,) * 8 + (hbm,) * 3,
        scratch_shapes=[
            pltpu.VMEM((dim, width), BF16),
            pltpu.VMEM((width, dim), BF16),
            pltpu.VMEM((dim, ff), BF16),
            pltpu.VMEM((ff, dim), BF16),
            pltpu.VMEM((own, dim), F32),
            pltpu.VMEM((heads * own, HD), BF16),
            pltpu.VMEM((nb, HD, block), BF16),
            pltpu.VMEM((nb, block, per * own), F32),
            pltpu.VMEM((chunks, n * rows, ff), BF16),
            pltpu.VMEM((chunks, n * rows, ff), BF16),
            pltpu.VMEM((nb, own, dim), BF16),
            *line_refs,
            *line_sems,
            dma((4,)),
            dma((n,)),
            dma((n,)),
            dma((3, chunks)),
            dma((nb,)),
            dma((nb,)),
        ],
        compiler_params=pltpu.CompilerParams(
            collective_id=1, has_side_effects=True, vmem_limit_bytes=67000000
        ),
    )(tokens, w_q, w_o, w_up, w_dn, w_kv, vecs, up_bias, pair_bias)


def from_behind(block, axis, distance):
    devices = range(lax.axis_size(axis))
    route = [(i - distance, i) for i in devices if i - distance in devices]
    return lax.ppermute(block, axis, route)


def layer_norm(values, gain_vec, bias_vec):
    row_mean = jnp.mean(values, axis=-1, keepdims=True)
    centred = values - row_mean
    row_var = jnp.mean(centred * centred, axis=-1, keepdims=True)
    return centred * lax.rsqrt(row_var + 1e-05) * gain_vec + bias_vec


def gelu_tanh(values):
    return jax.nn.gelu(values, approximate=True)


def t_dot(a, b):
    return lax.dot_general(a, b, (((0,), (0,)), ((), ())), preferred_element_type=F32)


def gather_rows(own_rows):
    return lax.all_gather(own_rows, "tensor", axis=0, tiled=True)


def sum_rows(partial):
    return lax.psum_scatter(
        partial.astype(BF16), "tensor", scatter_dimension=0, tiled=True
    ).astype(F32)


def swap(value, distance):
    size = lax.axis_size("dp")
    return lax.ppermute(value, "dp", [(i, i ^ distance) for i in range(size)])


def fold(value, distance, axis):
    bit = (lax.axis_index("dp") // distance) % 2
    half = value.shape[axis] // 2
    away = lax.dynamic_slice_in_dim(value, (1 - bit) * half, half, axis)
    kept = lax.dynamic_slice_in_dim(value, bit * half, half, axis)
    return kept + swap(away.astype(BF16), distance).astype(F32)


def unfold(value, distance, axis):
    bit = (lax.axis_index("dp") // distance) % 2
    other = swap(value, distance)
    low = jnp.where(bit == 0, value, other)
    high = jnp.where(bit == 0, other, value)
    return jnp.concatenate([low, high], axis=axis)


def sum_dp(value, axis, scatter=None):
    size = lax.axis_size("dp")
    distance = 1
    while distance < size:
        value = fold(value, distance, axis)
        if distance == 1 and scatter is not None:
            value = lax.psum_scatter(
                value.astype(BF16), "tensor", scatter_dimension=scatter, tiled=True
            ).astype(F32)
        distance *= 2
    value = value.astype(BF16)
    while distance > 1:
        distance //= 2
        value = unfold(value, distance, axis)
    return value.astype(F32)


def whole_weight(shard, split, join):
    size = lax.axis_size("dp")
    part = shard.shape[split] // size
    own = lax.dynamic_slice_in_dim(shard, lax.axis_index("dp") * part, part, split)
    own = lax.all_gather(own, "tensor", axis=join, tiled=True)
    return lax.all_gather(own, "dp", axis=split, tiled=True)


def on_device(
    tokens_in,
    cotangent,
    ln1_gain,
    ln1_bias,
    q_weight,
    q_bias,
    kv_weight,
    v_bias,
    o_weight,
    o_bias,
    ln2_gain,
    ln2_bias,
    up_weight,
    up_bias,
    down_weight,
    down_bias,
):
    section = lax.axis_index("section")
    tensor_count = lax.axis_size("tensor")
    tensor_rank = lax.axis_index("tensor")
    gain_one = ln1_gain[0].astype(F32)
    bias_one = ln1_bias[0].astype(F32)
    w_pairs = kv_weight[0]
    pair_bias = jnp.concatenate([jnp.zeros((HD,), F32), v_bias[0].astype(F32)])
    b_out = o_bias[0].astype(F32)
    gain_two = ln2_gain[0].astype(F32)
    bias_two = ln2_bias[0].astype(F32)
    w_up = up_weight[0]
    b_up = up_bias[0].astype(F32)
    w_down = down_weight[0]
    b_down = down_bias[0].astype(F32)
    blocks, own_count, seq_count, model_dim = tokens_in.shape
    assert seq_count == 1
    tokens_in = tokens_in[:, :, 0]
    cotangent = cotangent[:, :, 0]
    block_len = own_count * tensor_count
    total_len = blocks * block_len
    w_query = whole_weight(q_weight[0], 0, 1)
    w_out = whole_weight(o_weight[0], 1, 0)
    b_query = lax.all_gather(q_bias[0], "tensor", axis=0, tiled=True).astype(F32)
    heads = w_query.shape[1] // HD
    width = heads * HD
    ff_local = w_up.shape[1]
    score_scale = 1.0 / math.sqrt(HD)
    positions = jnp.arange(total_len, dtype=jnp.int32)

    def zeros(shape, dtype):
        return jnp.zeros(shape, dtype)

    def put(kept, value, index):
        return lax.dynamic_update_index_in_dim(kept, value, index, 0)

    def take(kept, index):
        return lax.dynamic_index_in_dim(kept, index, 0, keepdims=False)

    vecs = jnp.stack([gain_one, bias_one, gain_two, bias_two, b_out, b_down, b_query, b_query])
    (
        kept_normed,
        kept_query,
        kept_attended,
        kept_logsum,
        kept_input,
        kept_hidden,
        outputs,
        kv_cache,
        kept_normed_two,
        kept_active,
        kept_slope,
    ) = forward(
        tokens_in, w_query, w_out, w_up, w_down, w_pairs, vecs, b_up[None], pair_bias[None]
    )
    chunks, chunk_rows = kept_active.shape[1], own_count // kept_active.shape[1]
    kept_query = kept_query.reshape(blocks, heads, own_count, HD)
    kept_logsum = kept_logsum.reshape(blocks, heads, own_count)
    kept_input = kept_input.astype(F32)
    kept_normed_two = kept_normed_two.reshape(blocks, block_len, model_dim)
    kept_active = kept_active.reshape(blocks, block_len, ff_local)
    kept_slope = kept_slope.reshape(blocks, block_len, ff_local)

    def to_chunks(rows):
        rows = rows.reshape(tensor_count, chunks, chunk_rows, -1)
        return rows.transpose(1, 0, 2, 3).reshape(block_len, -1)

    def from_chunks(rows):
        rows = rows.reshape(chunks, tensor_count, chunk_rows, -1)
        return rows.transpose(1, 0, 2, 3).reshape(block_len, -1)

    key_rows = kv_cache[:, :HD]
    value_rows = kv_cache[:, HD:]
    kept_grad_mlp = zeros((blocks + 1, block_len, model_dim), BF16)
    kept_grad_pre = zeros((blocks + 1, block_len, ff_local), BF16)
    kept_branch = zeros((blocks + 1, own_count, model_dim), BF16)
    kept_grad_query = zeros((blocks + 1, own_count, width), BF16)
    kept_grad_pairs = zeros((blocks + 1, own_count, 2 * HD), BF16)
    input_grads = zeros((blocks + 1, own_count, model_dim), F32)
    pair_grad_acc = zeros((total_len, 2 * HD), F32)
    received_back = zeros((own_count, model_dim), F32)
    common = [zeros((model_dim,), F32) for _ in range(6)]
    for turn in range(blocks + 1):
        step_count = turn - (1 - section)
        valid = (step_count >= 0) & (step_count < blocks)
        block_index = blocks - 1 - jnp.clip(step_count, 0, blocks - 1)
        slot = jnp.where(valid, block_index, blocks)
        grad_out = jnp.where(section == 1, take(cotangent, block_index).astype(F32), received_back)
        grad_out = grad_out * valid.astype(F32)
        grad_mlp = to_chunks(gather_rows(grad_out.astype(BF16)))
        grad_active = dot_t(grad_mlp, w_down)
        grad_pre = (grad_active * take(kept_slope, block_index).astype(F32)).astype(BF16)
        grad_normed_two = sum_rows(from_chunks(dot_t(grad_pre, w_up)))
        norm_back_two = jax.vjp(layer_norm, take(kept_hidden, block_index), gain_two, bias_two)[1]
        grad_hidden_norm, gain_two_term, bias_two_term = norm_back_two(grad_normed_two)
        grad_hidden = grad_out + grad_hidden_norm
        branch = grad_hidden.astype(BF16)
        grad_attended = dot_t(branch, w_out).astype(BF16).reshape(own_count * heads, HD)
        query_rows = take(kept_query, block_index).transpose(1, 0, 2).reshape(own_count * heads, HD)
        log_total = take(kept_logsum, block_index).T.reshape(-1)
        visible = positions < (block_index + 1) * block_len
        scores = dot_t(query_rows, key_rows) * score_scale
        scores = jnp.where(visible, scores, -1e30)
        probabilities = jnp.exp(scores - log_total[:, None])
        grad_probs = dot_t(grad_attended, value_rows)
        row_inner = jnp.sum(probabilities * grad_probs, axis=-1, keepdims=True)
        grad_scores = (probabilities * (grad_probs - row_inner)).astype(BF16)
        grad_query = (dot(grad_scores, key_rows) * score_scale).astype(BF16)
        grad_query = grad_query.reshape(own_count, width)
        grad_keys = t_dot(grad_scores, query_rows) * score_scale
        grad_values = t_dot(probabilities.astype(BF16), grad_attended)
        pair_grad_acc = pair_grad_acc + jnp.concatenate([grad_keys, grad_values], axis=-1)
        block_pairs = lax.dynamic_slice_in_dim(pair_grad_acc, block_index * block_len, block_len, 0)
        grad_pairs = sum_rows(block_pairs).astype(BF16)
        grad_normed = dot_t(grad_query, w_query) + dot_t(grad_pairs, w_pairs)
        norm_back_one = jax.vjp(layer_norm, take(kept_input, block_index), gain_one, bias_one)[1]
        grad_input_norm, gain_one_term, bias_one_term = norm_back_one(grad_normed)
        grad_input = grad_hidden + grad_input_norm
        if turn < blocks:
            received_back = from_behind(grad_input.astype(BF16), "section", -1).astype(F32)
        scale = valid.astype(F32)
        terms = (
            gain_one_term * scale,
            bias_one_term * scale,
            jnp.sum(grad_hidden, axis=0),
            gain_two_term,
            bias_two_term,
            jnp.sum(grad_out, axis=0),
        )
        common = [total + term for total, term in zip(common, terms)]
        input_grads = put(input_grads, grad_input, slot)
        kept_grad_mlp = put(kept_grad_mlp, grad_mlp, slot)
        kept_grad_pre = put(kept_grad_pre, grad_pre, slot)
        kept_branch = put(kept_branch, branch, slot)
        kept_grad_query = put(kept_grad_query, grad_query, slot)
        kept_grad_pairs = put(kept_grad_pairs, grad_pairs, slot)

    def flat(kept):
        return kept[:blocks].reshape(-1, kept.shape[-1])

    down_w = t_dot(flat(kept_active), flat(kept_grad_mlp))
    up_w = t_dot(flat(kept_normed_two), flat(kept_grad_pre))
    up_b = jnp.sum(flat(kept_grad_pre).astype(F32), axis=0)
    out_w = t_dot(flat(kept_attended), flat(kept_branch))
    query_w = t_dot(flat(kept_normed), flat(kept_grad_query))
    query_b = jnp.sum(flat(kept_grad_query).astype(F32), axis=0)
    pair_w = t_dot(flat(kept_normed), flat(kept_grad_pairs))
    value_b = jnp.sum(flat(kept_grad_pairs)[:, HD:].astype(F32), axis=0)
    down_w = sum_dp(down_w, 0)
    up_w = sum_dp(up_w, 0)
    out_w = sum_dp(out_w, 1, 0)
    query_w = sum_dp(query_w, 0, 1)
    pair_w = lax.psum(pair_w.astype(BF16), ("tensor", "dp")).astype(F32)
    wide = jnp.zeros((tensor_count, ff_local), F32)
    wide = lax.dynamic_update_index_in_dim(wide, up_b, tensor_rank, 0)
    packed = jnp.concatenate([*common, query_b, value_b, wide.reshape(-1)])
    packed = lax.psum(packed, ("tensor", "dp"))
    vecs = packed[: 6 * model_dim].reshape(6, model_dim)
    own_query = lax.dynamic_slice_in_dim(
        packed, 6 * model_dim + tensor_rank * (width // tensor_count), width // tensor_count, 0
    )
    value_b = lax.slice_in_dim(packed, 6 * model_dim + width, 6 * model_dim + width + HD)
    own_up = lax.dynamic_slice_in_dim(
        packed, 6 * model_dim + width + HD + tensor_rank * ff_local, ff_local, 0
    )
    return (
        outputs[None, :, :, None],
        input_grads[None, :blocks, :, None],
        vecs[0][None],
        vecs[1][None],
        query_w[None],
        own_query[None],
        pair_w[None],
        value_b[None],
        out_w[None],
        vecs[2][None],
        vecs[3][None],
        vecs[4][None],
        up_w[None],
        own_up[None],
        down_w[None],
        vecs[5][None],
    )


def solution(mesh):
    placed = (
        P(None, "tensor", "dp", None),
        P(None, "tensor", "dp", None),
        P("section", None),
        P("section", None),
        P("section", None, "tensor"),
        P("section", "tensor"),
        P("section", None, None),
        P("section", None),
        P("section", "tensor", None),
        P("section", None),
        P("section", None),
        P("section", None),
        P("section", None, "tensor"),
        P("section", "tensor"),
        P("section", "tensor", None),
        P("section", None),
    )
    return jax.shard_map(
        on_device,
        mesh=mesh,
        in_specs=placed,
        out_specs=(
            P("section", None, "tensor", "dp", None),
            P("section", None, "tensor", "dp", None),
            P("section", None),
            P("section", None),
            P("section", None, "tensor"),
            P("section", "tensor"),
            P("section", None, None),
            P("section", None),
            P("section", "tensor", None),
            P("section", None),
            P("section", None),
            P("section", None),
            P("section", None, "tensor"),
            P("section", "tensor"),
            P("section", "tensor", None),
            P("section", None),
        ),
        check_vma=False,
    )
```

```python
import functools
import math

import jax
import jax.numpy as jnp
from jax import lax
from jax.experimental import pallas as pl
from jax.experimental.pallas import tpu as pltpu
from jax.sharding import PartitionSpec as P

HD = 128
F32 = jnp.float32
BF16 = jnp.bfloat16
MESH = pl.DeviceIdType.MESH
GELU_A = math.sqrt(2.0 / math.pi)
GELU_B = 0.044715


def dot(a, b):
    return jnp.dot(a, b, preferred_element_type=F32)


def dot_t(a, b):
    return lax.dot_general(a, b, (((1,), (1,)), ((), ())), preferred_element_type=F32)


def aligned(start, size):
    return pl.ds(pl.multiple_of(start, size), size)


def greet(n):
    me = lax.axis_index("tensor")
    barrier = pltpu.get_barrier_semaphore()
    for k in range(1, n):
        pl.semaphore_signal(
            barrier, inc=1, device_id={"tensor": lax.rem(me + k, n)}, device_id_type=MESH
        )
    pl.semaphore_signal(
        barrier, inc=1, device_id={"section": 1 - lax.axis_index("section")}, device_id_type=MESH
    )
    pl.semaphore_wait(barrier, n)


def normalize(v):
    mean = jnp.mean(v, axis=-1, keepdims=True)
    centred = v - mean
    var = jnp.mean(centred * centred, axis=-1, keepdims=True)
    rstd = lax.rsqrt(var + 1e-05)
    return centred * rstd, rstd


def line_rounds(n, chunks, rows, bufs, compute, finish):
    (g, terms, sum_r, sum_l, in_l, in_r) = bufs["refs"]
    (gs_r, gs_l, g_recv, rs_r, rs_l, rr_l, rr_r) = bufs["sems"]
    me = lax.axis_index("tensor")

    def part(j):
        return pl.ds(pl.multiple_of(j * rows, rows), rows)

    def gather_copy(c, j, step, to_right):
        return pltpu.make_async_remote_copy(
            src_ref=g.at[c, part(j)],
            dst_ref=g.at[c, part(j)],
            send_sem=(gs_r if to_right else gs_l).at[c, step],
            recv_sem=g_recv.at[c, j],
            device_id={"tensor": jnp.minimum(me + 1, n - 1) if to_right else jnp.maximum(me - 1, 0)},
            device_id_type=MESH,
        )

    def sum_copy(c, j, to_right):
        return pltpu.make_async_remote_copy(
            src_ref=(sum_r if to_right else sum_l).at[c, part(j)],
            dst_ref=(in_l if to_right else in_r).at[c, part(j)],
            send_sem=(rs_r if to_right else rs_l).at[c, j],
            recv_sem=(rr_l if to_right else rr_r).at[c, j],
            device_id={"tensor": jnp.minimum(me + 1, n - 1) if to_right else jnp.maximum(me - 1, 0)},
            device_id_type=MESH,
        )

    def slot(s, carry):
        for h in range(n):
            c = s - h

            @pl.when((c >= 0) & (c < chunks))
            def _(h=h, c=c):
                from_l = me - h >= 0
                from_r = me + h <= n - 1
                if h > 0:

                    @pl.when(from_l)
                    def _():
                        gather_copy(c, jnp.maximum(me - h, 0), 0, True).wait_recv()

                    @pl.when(from_r)
                    def _():
                        gather_copy(c, jnp.minimum(me + h, n - 1), 0, False).wait_recv()

                if h < n - 1:

                    @pl.when(from_l & (me < n - 1))
                    def _():
                        gather_copy(c, jnp.maximum(me - h, 0), h, True).start()

                    @pl.when(from_r & (me > 0))
                    def _():
                        gather_copy(c, jnp.minimum(me + h, n - 1), h, False).start()

        for h in range(n - 1):
            c = s - n - h

            @pl.when((c >= 0) & (c < chunks))
            def _(h=h, c=c):
                if h == 0:
                    finish(c, "kept")

                @pl.when((h >= me) & (me < n - 1))
                def _():
                    j = jnp.minimum(n - 1 - (h - me), n - 1)

                    @pl.when(me > 0)
                    def _():
                        sum_copy(c, j, True).wait_recv()
                        sum_r[c, part(j)] = (terms[c, part(j)] + in_l[c, part(j)].astype(F32)).astype(BF16)

                    @pl.when(me == 0)
                    def _():
                        sum_r[c, part(j)] = terms[c, part(j)].astype(BF16)

                    sum_copy(c, j, True).start()

                @pl.when((h >= n - 1 - me) & (me > 0))
                def _():
                    j = jnp.maximum(h - (n - 1 - me), 0)

                    @pl.when(me < n - 1)
                    def _():
                        sum_copy(c, j, False).wait_recv()
                        sum_l[c, part(j)] = (terms[c, part(j)] + in_r[c, part(j)].astype(F32)).astype(BF16)

                    @pl.when(me == n - 1)
                    def _():
                        sum_l[c, part(j)] = terms[c, part(j)].astype(BF16)

                    sum_copy(c, j, False).start()

        c_done = s - (2 * n - 1)

        @pl.when((c_done >= 0) & (c_done < chunks))
        def _():
            @pl.when(me > 0)
            def _():
                sum_copy(c_done, me, True).wait_recv()
                terms[c_done, part(me)] += in_l[c_done, part(me)].astype(F32)

            @pl.when(me < n - 1)
            def _():
                sum_copy(c_done, me, False).wait_recv()
                terms[c_done, part(me)] += in_r[c_done, part(me)].astype(F32)

        c_now = s - (n - 1)

        @pl.when((c_now >= 0) & (c_now < chunks))
        def _():
            compute(c_now)

        return carry

    lax.fori_loop(0, chunks + 2 * n - 1, slot, 0)

    def drain(c, carry):
        for h in range(n - 1):

            @pl.when((me - h >= 0) & (me < n - 1))
            def _(h=h):
                gather_copy(c, jnp.maximum(me - h, 0), h, True).wait_send()

            @pl.when((me + h <= n - 1) & (me > 0))
            def _(h=h):
                gather_copy(c, jnp.minimum(me + h, n - 1), h, False).wait_send()

        for j in range(n):

            @pl.when(j > me)
            def _(j=j):
                sum_copy(c, j, True).wait_send()

            @pl.when(j < me)
            def _(j=j):
                sum_copy(c, j, False).wait_send()

        return carry

    lax.fori_loop(0, chunks, drain, 0)


def line_scratch(n, chunks, rows, width):
    whole = n * rows
    refs = [
        pltpu.VMEM((chunks, whole, width), BF16),
        pltpu.VMEM((chunks, whole, width), F32),
    ] + [pltpu.VMEM((chunks, whole, width), BF16)] * 4
    sems = [pltpu.SemaphoreType.DMA((chunks, n))] * 7
    return refs, sems


def forward_kernel(
    cfg,
    tokens,
    w_q_hbm,
    w_o_hbm,
    w_up_hbm,
    w_dn_hbm,
    w_kv,
    vecs,
    up_bias,
    pair_bias,
    normed_out,
    query_out,
    att_out,
    lse_out,
    input_out,
    hidden_out,
    result_out,
    kv_out,
    two_hbm,
    act_hbm,
    slope_hbm,
    w_q,
    w_o,
    w_up,
    w_dn,
    x_ref,
    q_ref,
    v_t,
    s_ref,
    act,
    slope,
    inbox,
    g,
    terms,
    sum_r,
    sum_l,
    in_l,
    in_r,
    gs_r,
    gs_l,
    g_recv,
    rs_r,
    rs_l,
    rr_l,
    rr_r,
    w_sem,
    kv_send,
    kv_recv,
    keep_sem,
    hand_send,
    hand_recv,
):
    n, nb, own, chunks, rows, tile = (cfg[k] for k in ("n", "nb", "own", "chunks", "rows", "tile"))
    dim = x_ref.shape[1]
    ff = w_up.shape[1]
    width = w_q.shape[1]
    heads = width // HD
    block = n * own
    per = cfg["per"]
    me = lax.axis_index("tensor")
    sec = lax.axis_index("section")
    scale = 1.0 / math.sqrt(HD)
    loads = [
        pltpu.make_async_copy(src, dst, w_sem.at[k])
        for k, (src, dst) in enumerate(((w_q_hbm, w_q), (w_o_hbm, w_o), (w_up_hbm, w_up), (w_dn_hbm, w_dn)))
    ]
    for load in loads:
        load.start()
    greet(n)

    def pairs_copy(b, k):
        rows_here = aligned(b * block + me * own, own)
        return pltpu.make_async_remote_copy(
            src_ref=kv_out.at[rows_here],
            dst_ref=kv_out.at[rows_here],
            send_sem=kv_send.at[k],
            recv_sem=kv_recv.at[k],
            device_id={"tensor": lax.rem(me + k, n)},
            device_id_type=MESH,
        )

    def hand_copy(b):
        return pltpu.make_async_remote_copy(
            src_ref=result_out.at[b],
            dst_ref=inbox.at[b],
            send_sem=hand_send.at[b],
            recv_sem=hand_recv.at[b],
            device_id={"section": 1 - sec},
            device_id_type=MESH,
        )

    def keep_copies(b, c):
        return [
            pltpu.make_async_copy(g.at[c], two_hbm.at[b, c], keep_sem.at[0, c]),
            pltpu.make_async_copy(act.at[c], act_hbm.at[b, c], keep_sem.at[1, c]),
            pltpu.make_async_copy(slope.at[c], slope_hbm.at[b, c], keep_sem.at[2, c]),
        ]

    def block_step(b, carry):
        @pl.when(sec == 0)
        def _():
            input_out[b] = tokens[b]

        @pl.when(sec != 0)
        def _():
            hand_copy(b).wait_recv()
            input_out[b] = inbox[b]

        x_ref[...] = input_out[b].astype(F32)
        unit, _ = normalize(x_ref[...])
        normed = (unit * vecs[0:1] + vecs[1:2]).astype(BF16)
        normed_out[b] = normed
        pairs = (dot(normed, w_kv[...]) + pair_bias[...]).astype(BF16)
        kv_out[aligned(b * block + me * own, own)] = pairs
        for k in range(1, n):
            pairs_copy(b, k).start()

        @pl.when(b == 0)
        def _():
            loads[0].wait()

        def query_tile(t, carry):
            cols = aligned(t * tile, tile)
            q = (dot(normed_out[b], w_q[:, cols]) + vecs[6:7, cols]).astype(BF16)
            for k in range(tile // HD):
                q_ref[aligned((t * (tile // HD) + k) * own, own)] = q[:, k * HD : (k + 1) * HD]
            return carry

        lax.fori_loop(0, width // tile, query_tile, 0)
        query_out[b] = q_ref[...]
        for k in range(1, n):
            pairs_copy(b, k).wait_recv()
        here = aligned(b * block, block)
        v_t[b] = kv_out[here, HD:].astype(F32).T.astype(BF16)

        def head_tile(t, carry):
            q = q_ref[aligned(t * per * own, per * own)]

            def score(kb, top):
                s = dot_t(kv_out[aligned(kb * block, block), :HD], q) * scale
                s_ref[kb] = s
                return jnp.maximum(top, jnp.max(s, axis=0, keepdims=True))

            top = lax.fori_loop(0, b + 1, score, jnp.full((1, per * own), -jnp.inf, F32))

            def weigh(kb, state):
                total, acc = state
                e = jnp.exp(s_ref[kb] - top)
                return total + jnp.sum(e, axis=0, keepdims=True), acc + dot(v_t[kb], e.astype(BF16))

            total, acc = lax.fori_loop(
                0,
                b + 1,
                weigh,
                (jnp.zeros((1, per * own), F32), jnp.zeros((HD, per * own), F32)),
            )
            lse_out[b, t] = top + jnp.log(total)
            mixed = (acc / total).T.astype(BF16)
            for k in range(per):
                att_out[b, :, aligned((t * per + k) * HD, HD)] = mixed[k * own : (k + 1) * own]
            return carry

        lax.fori_loop(0, heads // per, head_tile, 0)

        @pl.when(b == 0)
        def _():
            loads[1].wait()

        def out_tile(t, carry):
            cols = aligned(t * tile, tile)
            hidden_out[b, :, cols] = (
                x_ref[:, cols] + dot(att_out[b], w_o[:, cols]) + vecs[4:5, cols]
            )
            return carry

        lax.fori_loop(0, dim // tile, out_tile, 0)
        unit, _ = normalize(hidden_out[b])
        normed_two = (unit * vecs[2:3] + vecs[3:4]).astype(BF16)
        for c in range(chunks):
            g[c, aligned(me * rows, rows)] = normed_two[c * rows : (c + 1) * rows]

        @pl.when(b == 0)
        def _():
            loads[2].wait()
            loads[3].wait()

        def compute(c):
            def up_tile(t, carry):
                cols = aligned(t * tile, tile)
                pre = dot(g[c], w_up[:, cols]) + up_bias[:, cols]
                inner = GELU_A * (pre + GELU_B * pre * pre * pre)
                th = jnp.tanh(inner)
                half = 0.5 * (1.0 + th)
                act[c, :, cols] = (pre * half).astype(BF16)
                slope[c, :, cols] = (
                    half + 0.5 * pre * (1.0 - th * th) * (GELU_A * (1.0 + 3.0 * GELU_B * pre * pre))
                ).astype(BF16)
                return carry

            lax.fori_loop(0, ff // tile, up_tile, 0)

            def down_tile(t, carry):
                cols = aligned(t * tile, tile)
                terms[c, :, cols] = dot(act[c], w_dn[:, cols])
                return carry

            lax.fori_loop(0, dim // tile, down_tile, 0)
            for copy in keep_copies(b, c):
                copy.start()

        def finish(c, what):
            for copy in keep_copies(b, c):
                copy.wait()

        line_rounds(
            n,
            chunks,
            rows,
            {
                "refs": (g, terms, sum_r, sum_l, in_l, in_r),
                "sems": (gs_r, gs_l, g_recv, rs_r, rs_l, rr_l, rr_r),
            },
            compute,
            finish,
        )
        for c in range(chunks):
            part = slice(c * rows, (c + 1) * rows)
            result_out[b, part] = (
                hidden_out[b, part] + terms[c, aligned(me * rows, rows)] + vecs[5:6]
            ).astype(BF16)

        @pl.when(sec == 0)
        def _():
            hand_copy(b).start()

        for k in range(1, n):
            pairs_copy(b, k).wait_send()
        return carry

    lax.fori_loop(0, nb, block_step, 0)

    def settle(b, carry):
        @pl.when(sec == 0)
        def _():
            hand_copy(b).wait_send()

        return carry

    lax.fori_loop(0, nb, settle, 0)


def forward(tokens, w_q, w_o, w_up, w_dn, w_kv, vecs, up_bias, pair_bias):
    n = lax.axis_size("tensor")
    nb, own, dim = tokens.shape
    rows = min(16, own)
    chunks = own // rows
    ff = w_up.shape[1]
    width = w_q.shape[1]
    heads = width // HD
    tile = min(512, dim, ff)
    per = min(heads, max(1, 256 // own))
    block = n * own
    cfg = dict(n=n, nb=nb, own=own, chunks=chunks, rows=rows, tile=tile, per=per)
    S = jax.ShapeDtypeStruct
    vmem = pl.BlockSpec(memory_space=pltpu.VMEM)
    hbm = pl.BlockSpec(memory_space=pl.ANY)
    line_refs, line_sems = line_scratch(n, chunks, rows, dim)
    dma = pltpu.SemaphoreType.DMA
    return pl.pallas_call(
        functools.partial(forward_kernel, cfg),
        name="forward",
        out_shape=(
            S((nb, own, dim), BF16),
            S((nb, heads * own, HD), BF16),
            S((nb, own, width), BF16),
            S((nb, heads // per, 1, per * own), F32),
            S((nb, own, dim), BF16),
            S((nb, own, dim), F32),
            S((nb, own, dim), BF16),
            S((nb * block, 2 * HD), BF16),
            S((nb, chunks, n * rows, dim), BF16),
            S((nb, chunks, n * rows, ff), BF16),
            S((nb, chunks, n * rows, ff), BF16),
        ),
        in_specs=[vmem, hbm, hbm, hbm, hbm, vmem, vmem, vmem, vmem],
        out_specs=(vmem,) * 8 + (hbm,) * 3,
        scratch_shapes=[
            pltpu.VMEM((dim, width), BF16),
            pltpu.VMEM((width, dim), BF16),
            pltpu.VMEM((dim, ff), BF16),
            pltpu.VMEM((ff, dim), BF16),
            pltpu.VMEM((own, dim), F32),
            pltpu.VMEM((heads * own, HD), BF16),
            pltpu.VMEM((nb, HD, block), BF16),
            pltpu.VMEM((nb, block, per * own), F32),
            pltpu.VMEM((chunks, n * rows, ff), BF16),
            pltpu.VMEM((chunks, n * rows, ff), BF16),
            pltpu.VMEM((nb, own, dim), BF16),
            *line_refs,
            *line_sems,
            dma((4,)),
            dma((n,)),
            dma((n,)),
            dma((3, chunks)),
            dma((nb,)),
            dma((nb,)),
        ],
        compiler_params=pltpu.CompilerParams(
            collective_id=1, has_side_effects=True, vmem_limit_bytes=67000000
        ),
    )(tokens, w_q, w_o, w_up, w_dn, w_kv, vecs, up_bias, pair_bias)


def norm_back(v, gain, grad):
    unit, rstd = normalize(v)
    scaled = grad * gain
    mean_one = jnp.mean(scaled, axis=-1, keepdims=True)
    mean_two = jnp.mean(scaled * unit, axis=-1, keepdims=True)
    back = rstd * (scaled - mean_one - unit * mean_two)
    return back, jnp.sum(grad * unit, axis=0, keepdims=True), jnp.sum(grad, axis=0, keepdims=True)


def backward_kernel(
    cfg,
    cot,
    inputs,
    hidden,
    query,
    lse,
    kv,
    vecs,
    w_kv,
    slope_hbm,
    w_dn_hbm,
    w_up_hbm,
    w_o_hbm,
    w_q_hbm,
    branch_out,
    gq_out,
    pairs_out,
    input_grad,
    common,
    up_sum,
    mlp_hbm,
    pre_hbm,
    w_dn,
    w_up,
    w_o,
    w_q,
    go,
    gn,
    slope,
    gpre,
    p_ref,
    g_ref,
    gk,
    gv,
    k_t,
    ga,
    inbox,
    hand,
    pair_send,
    pair_recv,
    g,
    terms,
    sum_r,
    sum_l,
    in_l,
    in_r,
    gs_r,
    gs_l,
    g_recv,
    rs_r,
    rs_l,
    rr_l,
    rr_r,
    w_sem,
    ps_sem,
    pr_sem,
    keep_sem,
    slope_sem,
    hand_send,
    hand_recv,
):
    n, nb, own, chunks, rows, tile = (cfg[k] for k in ("n", "nb", "own", "chunks", "rows", "tile"))
    per = cfg["per"]
    dim = go.shape[1]
    ff = w_up.shape[1]
    width = w_q.shape[1]
    heads = width // HD
    block = n * own
    me = lax.axis_index("tensor")
    sec = lax.axis_index("section")
    scale = 1.0 / math.sqrt(HD)
    loads = [
        pltpu.make_async_copy(src, dst, w_sem.at[k])
        for k, (src, dst) in enumerate(((w_dn_hbm, w_dn), (w_up_hbm, w_up), (w_o_hbm, w_o), (w_q_hbm, w_q)))
    ]
    for load in loads:
        load.start()
    greet(n)
    gk[...] = jnp.zeros_like(gk)
    gv[...] = jnp.zeros_like(gv)
    common[...] = jnp.zeros_like(common)
    up_sum[...] = jnp.zeros_like(up_sum)
    for kb in range(nb):
        k_t[kb] = kv[kb * block : (kb + 1) * block, :HD].astype(F32).T.astype(BF16)

    def pair_copy(k):
        target = lax.rem(me + k, n)
        return pltpu.make_async_remote_copy(
            src_ref=pair_send.at[aligned(target * own, own)],
            dst_ref=pair_recv.at[k],
            send_sem=ps_sem.at[k],
            recv_sem=pr_sem.at[k],
            device_id={"tensor": target},
            device_id_type=MESH,
        )

    def hand_copy(b):
        return pltpu.make_async_remote_copy(
            src_ref=hand,
            dst_ref=inbox.at[b],
            send_sem=hand_send,
            recv_sem=hand_recv.at[b],
            device_id={"section": 1 - sec},
            device_id_type=MESH,
        )

    def keep_copies(b, c):
        return [
            pltpu.make_async_copy(g.at[c], mlp_hbm.at[b, c], keep_sem.at[0, c]),
            pltpu.make_async_copy(gpre.at[c], pre_hbm.at[b, c], keep_sem.at[1, c]),
        ]

    def block_step(i, carry):
        b = nb - 1 - i
        slope_load = pltpu.make_async_copy(slope_hbm.at[b], slope, slope_sem)
        slope_load.start()

        @pl.when(sec == 1)
        def _():
            go[...] = cot[b].astype(F32)

        @pl.when(sec != 1)
        def _():
            hand_copy(b).wait_recv()
            go[...] = inbox[b].astype(F32)

        common[5:6, :dim] += jnp.sum(go[...], axis=0, keepdims=True)
        for c in range(chunks):
            g[c, aligned(me * rows, rows)] = go[c * rows : (c + 1) * rows].astype(BF16)
        slope_load.wait()

        @pl.when(i == 0)
        def _():
            loads[0].wait()
            loads[1].wait()

        def compute(c):
            def act_tile(t, carry):
                cols = aligned(t * tile, tile)
                grad = (dot_t(g[c], w_dn[cols]) * slope[c, :, cols].astype(F32)).astype(BF16)
                gpre[c, :, cols] = grad
                up_sum[:, cols] += jnp.sum(grad.astype(F32), axis=0, keepdims=True)
                return carry

            lax.fori_loop(0, ff // tile, act_tile, 0)

            def back_tile(t, carry):
                cols = aligned(t * tile, tile)
                terms[c, :, cols] = dot_t(gpre[c], w_up[cols])
                return carry

            lax.fori_loop(0, dim // tile, back_tile, 0)
            for copy in keep_copies(b, c):
                copy.start()

        def finish(c, what):
            for copy in keep_copies(b, c):
                copy.wait()

        line_rounds(
            n,
            chunks,
            rows,
            {
                "refs": (g, terms, sum_r, sum_l, in_l, in_r),
                "sems": (gs_r, gs_l, g_recv, rs_r, rs_l, rr_l, rr_r),
            },
            compute,
            finish,
        )
        for c in range(chunks):
            gn[c * rows : (c + 1) * rows] = terms[c, aligned(me * rows, rows)]
        back, gain_sum, bias_sum = norm_back(hidden[b], vecs[2:3], gn[...])
        common[3:4, :dim] += gain_sum
        common[4:5, :dim] += bias_sum
        go[...] += back
        common[2:3, :dim] += jnp.sum(go[...], axis=0, keepdims=True)
        branch_out[b] = go[...].astype(BF16)

        @pl.when(i == 0)
        def _():
            loads[2].wait()

        def att_tile(t, carry):
            grad = dot_t(branch_out[b], w_o[aligned(t * tile, tile)]).astype(BF16)
            for k in range(tile // HD):
                ga[aligned((t * (tile // HD) + k) * own, own)] = grad[:, k * HD : (k + 1) * HD]
            return carry

        lax.fori_loop(0, width // tile, att_tile, 0)

        def head_tile(t, carry):
            here = aligned(t * per * own, per * own)
            q = query[b, here]
            grad = ga[here]
            log_total = lse[b, t]

            def first(kb, inner):
                keys = aligned(kb * block, block)
                prob = jnp.exp(dot_t(kv[keys, :HD], q) * scale - log_total)
                grad_prob = dot_t(kv[keys, HD:], grad)
                p_ref[kb] = prob
                g_ref[kb] = grad_prob
                return inner + jnp.sum(prob * grad_prob, axis=0, keepdims=True)

            inner = lax.fori_loop(0, b + 1, first, jnp.zeros((1, per * own), F32))

            def second(kb, acc):
                keys = aligned(kb * block, block)
                prob = p_ref[kb]
                grad_score = (prob * (g_ref[kb] - inner)).astype(BF16)
                gk[keys] += dot(grad_score, q)
                gv[keys] += dot(prob.astype(BF16), grad)
                return acc + dot(k_t[kb], grad_score)

            acc = lax.fori_loop(0, b + 1, second, jnp.zeros((HD, per * own), F32))
            back = (acc * scale).T.astype(BF16)
            for k in range(per):
                gq_out[b, :, aligned((t * per + k) * HD, HD)] = back[k * own : (k + 1) * own]
            return carry

        lax.fori_loop(0, heads // per, head_tile, 0)
        here = aligned(b * block, block)
        pair_send[:, :HD] = (gk[here] * scale).astype(BF16)
        pair_send[:, HD:] = gv[here].astype(BF16)
        for k in range(1, n):
            pair_copy(k).start()
        common[6:7, :width] += jnp.sum(gq_out[b].astype(F32), axis=0, keepdims=True)

        @pl.when(i == 0)
        def _():
            loads[3].wait()

        def normed_tile(t, carry):
            cols = aligned(t * tile, tile)
            gn[:, cols] = dot_t(gq_out[b], w_q[cols])
            return carry

        lax.fori_loop(0, dim // tile, normed_tile, 0)
        mine = aligned(b * block + me * own, own)
        total_k = gk[mine] * scale
        total_v = gv[mine]
        for k in range(1, n):
            pair_copy(k).wait_recv()
            total_k += pair_recv[k, :, :HD].astype(F32)
            total_v += pair_recv[k, :, HD:].astype(F32)
        pairs_out[b, :, :HD] = total_k.astype(BF16)
        pairs_out[b, :, HD:] = total_v.astype(BF16)
        common[7:8, : 2 * HD] += jnp.sum(pairs_out[b].astype(F32), axis=0, keepdims=True)

        def pair_tile(t, carry):
            cols = aligned(t * tile, tile)
            gn[:, cols] += dot_t(pairs_out[b], w_kv[cols])
            return carry

        lax.fori_loop(0, dim // tile, pair_tile, 0)
        back, gain_sum, bias_sum = norm_back(inputs[b].astype(F32), vecs[0:1], gn[...])
        common[0:1, :dim] += gain_sum
        common[1:2, :dim] += bias_sum
        go[...] += back
        input_grad[b] = go[...]
        for k in range(1, n):
            pair_copy(k).wait_send()

        @pl.when(sec == 1)
        def _():
            @pl.when(i > 0)
            def _():
                hand_copy(b).wait_send()

            hand[...] = go[...].astype(BF16)
            hand_copy(b).start()

        return carry

    lax.fori_loop(0, nb, block_step, 0)

    @pl.when(sec == 1)
    def _():
        hand_copy(0).wait_send()


def backward(cot, inputs, hidden, query, lse, kv, vecs, w_kv, slope, w_dn, w_up, w_o, w_q):
    n = lax.axis_size("tensor")
    nb, own, dim = cot.shape
    chunks, rows = slope.shape[1], own // slope.shape[1]
    ff = w_up.shape[1]
    width = w_q.shape[1]
    heads = width // HD
    tile = min(512, dim, ff)
    per = lse.shape[3] // own
    block = n * own
    cfg = dict(n=n, nb=nb, own=own, chunks=chunks, rows=rows, tile=tile, per=per)
    S = jax.ShapeDtypeStruct
    vmem = pl.BlockSpec(memory_space=pltpu.VMEM)
    hbm = pl.BlockSpec(memory_space=pl.ANY)
    line_refs, line_sems = line_scratch(n, chunks, rows, dim)
    dma = pltpu.SemaphoreType.DMA
    return pl.pallas_call(
        functools.partial(backward_kernel, cfg),
        name="backward",
        out_shape=(
            S((nb, own, dim), BF16),
            S((nb, own, width), BF16),
            S((nb, own, 2 * HD), BF16),
            S((nb, own, dim), F32),
            S((8, max(dim, width)), F32),
            S((1, ff), F32),
            S((nb, chunks, n * rows, dim), BF16),
            S((nb, chunks, n * rows, ff), BF16),
        ),
        in_specs=[vmem] * 8 + [hbm] * 5,
        out_specs=(vmem,) * 6 + (hbm,) * 2,
        scratch_shapes=[
            pltpu.VMEM((ff, dim), BF16),
            pltpu.VMEM((dim, ff), BF16),
            pltpu.VMEM((width, dim), BF16),
            pltpu.VMEM((dim, width), BF16),
            pltpu.VMEM((own, dim), F32),
            pltpu.VMEM((own, dim), F32),
            pltpu.VMEM((chunks, n * rows, ff), BF16),
            pltpu.VMEM((chunks, n * rows, ff), BF16),
            pltpu.VMEM((nb, block, per * own), F32),
            pltpu.VMEM((nb, block, per * own), F32),
            pltpu.VMEM((nb * block, HD), F32),
            pltpu.VMEM((nb * block, HD), F32),
            pltpu.VMEM((nb, HD, block), BF16),
            pltpu.VMEM((heads * own, HD), BF16),
            pltpu.VMEM((nb, own, dim), BF16),
            pltpu.VMEM((own, dim), BF16),
            pltpu.VMEM((block, 2 * HD), BF16),
            pltpu.VMEM((n, own, 2 * HD), BF16),
            *line_refs,
            *line_sems,
            dma((4,)),
            dma((n,)),
            dma((n,)),
            dma((2, chunks)),
            dma(()),
            dma(()),
            dma((nb,)),
        ],
        compiler_params=pltpu.CompilerParams(
            collective_id=2, has_side_effects=True, vmem_limit_bytes=67000000
        ),
    )(cot, inputs, hidden, query, lse, kv, vecs, w_kv, slope, w_dn, w_up, w_o, w_q)


def t_dot(a, b):
    return lax.dot_general(a, b, (((0,), (0,)), ((), ())), preferred_element_type=F32)


def swap(value, distance):
    size = lax.axis_size("dp")
    return lax.ppermute(value, "dp", [(i, i ^ distance) for i in range(size)])


def fold(value, distance, axis):
    bit = (lax.axis_index("dp") // distance) % 2
    half = value.shape[axis] // 2
    away = lax.dynamic_slice_in_dim(value, (1 - bit) * half, half, axis)
    kept = lax.dynamic_slice_in_dim(value, bit * half, half, axis)
    return kept + swap(away.astype(BF16), distance).astype(F32)


def unfold(value, distance, axis):
    bit = (lax.axis_index("dp") // distance) % 2
    other = swap(value, distance)
    low = jnp.where(bit == 0, value, other)
    high = jnp.where(bit == 0, other, value)
    return jnp.concatenate([low, high], axis=axis)


def sum_dp(value, axis, scatter=None):
    size = lax.axis_size("dp")
    distance = 1
    while distance < size:
        value = fold(value, distance, axis)
        if distance == 1 and scatter is not None:
            value = lax.psum_scatter(
                value.astype(BF16), "tensor", scatter_dimension=scatter, tiled=True
            ).astype(F32)
        distance *= 2
    value = value.astype(BF16)
    while distance > 1:
        distance //= 2
        value = unfold(value, distance, axis)
    return value.astype(F32)


def whole_weight(shard, split, join):
    size = lax.axis_size("dp")
    part = shard.shape[split] // size
    own = lax.dynamic_slice_in_dim(shard, lax.axis_index("dp") * part, part, split)
    own = lax.all_gather(own, "tensor", axis=join, tiled=True)
    return lax.all_gather(own, "dp", axis=split, tiled=True)


def on_device(
    tokens_in,
    cotangent,
    ln1_gain,
    ln1_bias,
    q_weight,
    q_bias,
    kv_weight,
    v_bias,
    o_weight,
    o_bias,
    ln2_gain,
    ln2_bias,
    up_weight,
    up_bias,
    down_weight,
    down_bias,
):
    tensor_count = lax.axis_size("tensor")
    tensor_rank = lax.axis_index("tensor")
    gain_one = ln1_gain[0].astype(F32)
    bias_one = ln1_bias[0].astype(F32)
    w_pairs = kv_weight[0]
    pair_bias = jnp.concatenate([jnp.zeros((HD,), F32), v_bias[0].astype(F32)])
    b_out = o_bias[0].astype(F32)
    gain_two = ln2_gain[0].astype(F32)
    bias_two = ln2_bias[0].astype(F32)
    w_up = up_weight[0]
    b_up = up_bias[0].astype(F32)
    w_down = down_weight[0]
    b_down = down_bias[0].astype(F32)
    blocks, own_count, seq_count, model_dim = tokens_in.shape
    assert seq_count == 1
    tokens_in = tokens_in[:, :, 0]
    cotangent = cotangent[:, :, 0]
    w_query = whole_weight(q_weight[0], 0, 1)
    w_out = whole_weight(o_weight[0], 1, 0)
    b_query = lax.all_gather(q_bias[0], "tensor", axis=0, tiled=True).astype(F32)
    width = w_query.shape[1]
    ff_local = w_up.shape[1]

    vecs = jnp.stack([gain_one, bias_one, gain_two, bias_two, b_out, b_down, b_query, b_query])
    (
        kept_normed,
        kept_query,
        kept_attended,
        kept_logsum,
        kept_input,
        kept_hidden,
        outputs,
        kv_cache,
        kept_normed_two,
        kept_active,
        kept_slope,
    ) = forward(
        tokens_in, w_query, w_out, w_up, w_down, w_pairs, vecs, b_up[None], pair_bias[None]
    )
    (
        kept_branch,
        kept_grad_query,
        kept_grad_pairs,
        input_grads,
        common,
        up_b,
        kept_grad_mlp,
        kept_grad_pre,
    ) = backward(
        cotangent,
        kept_input,
        kept_hidden,
        kept_query,
        kept_logsum,
        kv_cache,
        vecs,
        w_pairs,
        kept_slope,
        w_down,
        w_up,
        w_out,
        w_query,
    )

    def flat(kept):
        return kept.reshape(-1, kept.shape[-1])

    down_w = t_dot(flat(kept_active), flat(kept_grad_mlp))
    up_w = t_dot(flat(kept_normed_two), flat(kept_grad_pre))
    out_w = t_dot(flat(kept_attended), flat(kept_branch))
    query_w = t_dot(flat(kept_normed), flat(kept_grad_query))
    pair_w = t_dot(flat(kept_normed), flat(kept_grad_pairs))
    down_w = sum_dp(down_w, 0)
    up_w = sum_dp(up_w, 0)
    out_w = sum_dp(out_w, 1, 0)
    query_w = sum_dp(query_w, 0, 1)
    pair_w = lax.psum(pair_w.astype(BF16), ("tensor", "dp")).astype(F32)
    wide = jnp.zeros((tensor_count, ff_local), F32)
    wide = lax.dynamic_update_index_in_dim(wide, up_b[0], tensor_rank, 0)
    packed = jnp.concatenate(
        [common[:6, :model_dim].reshape(-1), common[6, :width], common[7, HD : 2 * HD], wide.reshape(-1)]
    )
    packed = lax.psum(packed, ("tensor", "dp"))
    vecs = packed[: 6 * model_dim].reshape(6, model_dim)
    own_query = lax.dynamic_slice_in_dim(
        packed, 6 * model_dim + tensor_rank * (width // tensor_count), width // tensor_count, 0
    )
    value_b = lax.slice_in_dim(packed, 6 * model_dim + width, 6 * model_dim + width + HD)
    own_up = lax.dynamic_slice_in_dim(
        packed, 6 * model_dim + width + HD + tensor_rank * ff_local, ff_local, 0
    )
    return (
        outputs[None, :, :, None],
        input_grads[None, :, :, None],
        vecs[0][None],
        vecs[1][None],
        query_w[None],
        own_query[None],
        pair_w[None],
        value_b[None],
        out_w[None],
        vecs[2][None],
        vecs[3][None],
        vecs[4][None],
        up_w[None],
        own_up[None],
        down_w[None],
        vecs[5][None],
    )


def solution(mesh):
    placed = (
        P(None, "tensor", "dp", None),
        P(None, "tensor", "dp", None),
        P("section", None),
        P("section", None),
        P("section", None, "tensor"),
        P("section", "tensor"),
        P("section", None, None),
        P("section", None),
        P("section", "tensor", None),
        P("section", None),
        P("section", None),
        P("section", None),
        P("section", None, "tensor"),
        P("section", "tensor"),
        P("section", "tensor", None),
        P("section", None),
    )
    return jax.shard_map(
        on_device,
        mesh=mesh,
        in_specs=placed,
        out_specs=(
            P("section", None, "tensor", "dp", None),
            P("section", None, "tensor", "dp", None),
            P("section", None),
            P("section", None),
            P("section", None, "tensor"),
            P("section", "tensor"),
            P("section", None, None),
            P("section", None),
            P("section", "tensor", None),
            P("section", None),
            P("section", None),
            P("section", None),
            P("section", None, "tensor"),
            P("section", "tensor"),
            P("section", "tensor", None),
            P("section", None),
        ),
        check_vma=False,
    )
```

```python
import functools
import math

import jax
import jax.numpy as jnp
from jax import lax
from jax.experimental import pallas as pl
from jax.experimental.pallas import tpu as pltpu
from jax.sharding import PartitionSpec as P

HD = 128
F32 = jnp.float32
BF16 = jnp.bfloat16
MESH = pl.DeviceIdType.MESH
GELU_A = math.sqrt(2.0 / math.pi)
GELU_B = 0.044715


def dot(a, b):
    return jnp.dot(a, b, preferred_element_type=F32)


def dot_t(a, b):
    return lax.dot_general(a, b, (((1,), (1,)), ((), ())), preferred_element_type=F32)


def aligned(start, size):
    return pl.ds(pl.multiple_of(start, size), size)


def greet(n):
    me, d = lax.axis_index("tensor"), lax.axis_index("dp")
    dp = lax.axis_size("dp")
    barrier = pltpu.get_barrier_semaphore()
    for k in range(1, n):
        pl.semaphore_signal(
            barrier, inc=1, device_id={"tensor": lax.rem(me + k, n)}, device_id_type=MESH
        )
    for k in range(1, dp):
        pl.semaphore_signal(
            barrier, inc=1, device_id={"dp": lax.rem(d + k, dp)}, device_id_type=MESH
        )
    pl.semaphore_signal(
        barrier, inc=1, device_id={"section": 1 - lax.axis_index("section")}, device_id_type=MESH
    )
    pl.semaphore_wait(barrier, n + dp - 1)


def gather_weight(n, whole, piece, recv, sends):
    z_recv, x_recv, c_recv = recv
    s_r, s_l, s_x, s_c, s_cx = sends
    me, d = lax.axis_index("tensor"), lax.axis_index("dp")
    dp = lax.axis_size("dp")
    peers = dp // 2
    partner = d + 1 - 2 * lax.rem(d, 2)

    def copy(rank, j, send, recv, device):
        ref = piece(whole, rank, j)
        return pltpu.make_async_remote_copy(
            src_ref=ref, dst_ref=ref, send_sem=send, recv_sem=recv, device_id=device, device_id_type=MESH
        )

    def along(j, h, to_right):
        target = jnp.minimum(me + 1, n - 1) if to_right else jnp.maximum(me - 1, 0)
        return copy(d, j, (s_r if to_right else s_l).at[h], z_recv.at[j], {"tensor": target})

    def across(rank, k, j):
        return copy(rank, j, s_x.at[k, j], x_recv.at[k, j], {"dp": lax.rem(d + 2 * k, dp)})

    def on_chip(rank, k, j):
        return copy(rank, j, (s_c if k == 0 else s_cx).at[k, j], c_recv.at[k, j], {"dp": partner})

    def arrivals(h):
        return ((me - h >= 0, jnp.maximum(me - h, 0), True), (me + h <= n - 1, jnp.minimum(me + h, n - 1), False))

    for h in range(n):
        for there, j, to_right in arrivals(h):
            onward = (me < n - 1) if to_right else (me > 0)
            if h > 0:

                @pl.when(there)
                def _(j=j, h=h, to_right=to_right):
                    along(j, 0, to_right).wait_recv()

            if h < n - 1:

                @pl.when(there & onward)
                def _(j=j, h=h, to_right=to_right):
                    along(j, h, to_right).start()

            if h > 0:

                @pl.when(there)
                def _(j=j):
                    for k in range(1, peers):
                        across(d, k, j).start()
                    on_chip(d, 0, j).start()

    def relay():
        for h in range(1, n):
            for there, j, _ in arrivals(h):

                @pl.when(there)
                def _(j=j):
                    for k in range(1, peers):
                        rank = lax.rem(d + dp - 2 * k, dp)
                        across(rank, k, j).wait_recv()
                        on_chip(rank, k, j).start()

    def complete():
        for h in range(1, n):
            for there, j, _ in arrivals(h):

                @pl.when(there)
                def _(j=j):
                    for k in range(peers):
                        rank = lax.rem(partner + dp - 2 * k, dp)
                        on_chip(rank, k, j).wait_recv()

    def drain():
        for h in range(n):
            for there, j, to_right in arrivals(h):
                onward = (me < n - 1) if to_right else (me > 0)
                if h < n - 1:

                    @pl.when(there & onward)
                    def _(j=j, h=h, to_right=to_right):
                        along(j, h, to_right).wait_send()

                if h > 0:

                    @pl.when(there)
                    def _(j=j):
                        for k in range(1, peers):
                            across(d, k, j).wait_send()
                        for k in range(peers):
                            on_chip(d, k, j).wait_send()

    return relay, complete, drain


def normalize(v):
    mean = jnp.mean(v, axis=-1, keepdims=True)
    centred = v - mean
    var = jnp.mean(centred * centred, axis=-1, keepdims=True)
    rstd = lax.rsqrt(var + 1e-05)
    return centred * rstd, rstd


def line_rounds(n, chunks, rows, bufs, compute, finish):
    (g, terms, sum_r, sum_l, in_l, in_r) = bufs["refs"]
    (gs_r, gs_l, g_recv, rs_r, rs_l, rr_l, rr_r) = bufs["sems"]
    me = lax.axis_index("tensor")

    def part(j):
        return pl.ds(pl.multiple_of(j * rows, rows), rows)

    def gather_copy(c, j, step, to_right):
        return pltpu.make_async_remote_copy(
            src_ref=g.at[c, part(j)],
            dst_ref=g.at[c, part(j)],
            send_sem=(gs_r if to_right else gs_l).at[c, step],
            recv_sem=g_recv.at[c, j],
            device_id={"tensor": jnp.minimum(me + 1, n - 1) if to_right else jnp.maximum(me - 1, 0)},
            device_id_type=MESH,
        )

    def sum_copy(c, j, to_right):
        return pltpu.make_async_remote_copy(
            src_ref=(sum_r if to_right else sum_l).at[c, part(j)],
            dst_ref=(in_l if to_right else in_r).at[c, part(j)],
            send_sem=(rs_r if to_right else rs_l).at[c, j],
            recv_sem=(rr_l if to_right else rr_r).at[c, j],
            device_id={"tensor": jnp.minimum(me + 1, n - 1) if to_right else jnp.maximum(me - 1, 0)},
            device_id_type=MESH,
        )

    def slot(s, carry):
        for h in range(n):
            c = s - h

            @pl.when((c >= 0) & (c < chunks))
            def _(h=h, c=c):
                from_l = me - h >= 0
                from_r = me + h <= n - 1
                if h > 0:

                    @pl.when(from_l)
                    def _():
                        gather_copy(c, jnp.maximum(me - h, 0), 0, True).wait_recv()

                    @pl.when(from_r)
                    def _():
                        gather_copy(c, jnp.minimum(me + h, n - 1), 0, False).wait_recv()

                if h < n - 1:

                    @pl.when(from_l & (me < n - 1))
                    def _():
                        gather_copy(c, jnp.maximum(me - h, 0), h, True).start()

                    @pl.when(from_r & (me > 0))
                    def _():
                        gather_copy(c, jnp.minimum(me + h, n - 1), h, False).start()

        for h in range(n - 1):
            c = s - n - h

            @pl.when((c >= 0) & (c < chunks))
            def _(h=h, c=c):
                if h == 0:
                    finish(c, "kept")

                @pl.when((h >= me) & (me < n - 1))
                def _():
                    j = jnp.minimum(n - 1 - (h - me), n - 1)

                    @pl.when(me > 0)
                    def _():
                        sum_copy(c, j, True).wait_recv()
                        sum_r[c, part(j)] = (terms[c, part(j)] + in_l[c, part(j)].astype(F32)).astype(BF16)

                    @pl.when(me == 0)
                    def _():
                        sum_r[c, part(j)] = terms[c, part(j)].astype(BF16)

                    sum_copy(c, j, True).start()

                @pl.when((h >= n - 1 - me) & (me > 0))
                def _():
                    j = jnp.maximum(h - (n - 1 - me), 0)

                    @pl.when(me < n - 1)
                    def _():
                        sum_copy(c, j, False).wait_recv()
                        sum_l[c, part(j)] = (terms[c, part(j)] + in_r[c, part(j)].astype(F32)).astype(BF16)

                    @pl.when(me == n - 1)
                    def _():
                        sum_l[c, part(j)] = terms[c, part(j)].astype(BF16)

                    sum_copy(c, j, False).start()

        c_done = s - (2 * n - 1)

        @pl.when((c_done >= 0) & (c_done < chunks))
        def _():
            @pl.when(me > 0)
            def _():
                sum_copy(c_done, me, True).wait_recv()
                terms[c_done, part(me)] += in_l[c_done, part(me)].astype(F32)

            @pl.when(me < n - 1)
            def _():
                sum_copy(c_done, me, False).wait_recv()
                terms[c_done, part(me)] += in_r[c_done, part(me)].astype(F32)

        c_now = s - (n - 1)

        @pl.when((c_now >= 0) & (c_now < chunks))
        def _():
            compute(c_now)

        return carry

    lax.fori_loop(0, chunks + 2 * n - 1, slot, 0)

    def drain(c, carry):
        for h in range(n - 1):

            @pl.when((me - h >= 0) & (me < n - 1))
            def _(h=h):
                gather_copy(c, jnp.maximum(me - h, 0), h, True).wait_send()

            @pl.when((me + h <= n - 1) & (me > 0))
            def _(h=h):
                gather_copy(c, jnp.minimum(me + h, n - 1), h, False).wait_send()

        for j in range(n):

            @pl.when(j > me)
            def _(j=j):
                sum_copy(c, j, True).wait_send()

            @pl.when(j < me)
            def _(j=j):
                sum_copy(c, j, False).wait_send()

        return carry

    lax.fori_loop(0, chunks, drain, 0)


def line_scratch(n, chunks, rows, width):
    whole = n * rows
    refs = [
        pltpu.VMEM((chunks, whole, width), BF16),
        pltpu.VMEM((chunks, whole, width), F32),
    ] + [pltpu.VMEM((chunks, whole, width), BF16)] * 4
    sems = [pltpu.SemaphoreType.DMA((chunks, n))] * 7
    return refs, sems


def forward_kernel(
    cfg,
    tokens,
    q_hbm,
    o_hbm,
    w_up_hbm,
    w_dn_hbm,
    w_kv,
    vecs,
    q_bias,
    up_bias,
    pair_bias,
    query_out,
    lse_out,
    input_out,
    hidden_out,
    result_out,
    kv_out,
    two_hbm,
    act_hbm,
    slope_hbm,
    normed_all,
    att_all,
    q_whole,
    o_whole,
    normed_out,
    att_out,
    bias_q,
    w_q,
    w_o,
    w_up,
    w_dn,
    x_ref,
    q_ref,
    v_t,
    s_ref,
    act,
    slope,
    inbox,
    g,
    terms,
    sum_r,
    sum_l,
    in_l,
    in_r,
    gs_r,
    gs_l,
    g_recv,
    rs_r,
    rs_l,
    rr_l,
    rr_r,
    w_sem,
    kv_send,
    kv_recv,
    keep_sem,
    hand_send,
    hand_recv,
    wz_recv,
    wx_recv,
    wc_recv,
    wz_right,
    wz_left,
    wx_send,
    wc_send,
    wcx_send,
    bias_send,
    bias_recv,
    rows_send,
    rows_recv,
    own_sem,
    swap_send,
    swap_recv,
):
    n, nb, own, chunks, rows, tile = (cfg[k] for k in ("n", "nb", "own", "chunks", "rows", "tile"))
    dp = lax.axis_size("dp")
    d = lax.axis_index("dp")
    peers, mine = dp // 2, d // 2
    dim = x_ref.shape[1]
    share = bias_q.shape[2]
    q_tile = min(tile, share)
    ff = w_up.shape[1]
    width = w_q.shape[1]
    heads = width // HD
    block = n * own
    per = cfg["per"]
    me = lax.axis_index("tensor")
    sec = lax.axis_index("section")
    scale = 1.0 / math.sqrt(HD)
    loads = [
        pltpu.make_async_copy(src, dst, w_sem.at[k])
        for k, (src, dst) in enumerate(
            (
                (q_hbm, w_q.at[:, aligned(me * share, share)]),
                (o_hbm, w_o.at[aligned(me * share, share)]),
                (w_up_hbm, w_up),
                (w_dn_hbm, w_dn),
            )
        )
    ]
    for load in loads:
        load.start()
    greet(n)

    def q_piece(ref, rank, j):
        return ref.at[aligned(rank * (dim // dp), dim // dp), aligned(j * share, share)]

    def o_piece(ref, rank, j):
        return ref.at[aligned(j * share + rank * (share // dp), share // dp)]

    def bias_copy(k):
        return pltpu.make_async_remote_copy(
            src_ref=q_bias,
            dst_ref=bias_q.at[me],
            send_sem=bias_send.at[k],
            recv_sem=bias_recv.at[k],
            device_id={"tensor": lax.rem(me + k, n)},
            device_id_type=MESH,
        )

    bias_q[me] = q_bias[...]
    for k in range(1, n):
        bias_copy(k).start()
    loads[0].wait()
    loads[1].wait()
    gathers = []
    for m, (whole, piece) in enumerate(((w_q, q_piece), (w_o, o_piece))):
        gathers.append(
            gather_weight(
                n,
                whole,
                piece,
                (wz_recv.at[m], wx_recv.at[m], wc_recv.at[m]),
                (wz_right.at[m], wz_left.at[m], wx_send.at[m], wc_send.at[m], wcx_send.at[m]),
            )
        )
    for relay, complete, drain in gathers:
        relay()
    for relay, complete, drain in gathers:
        complete()
    stores = [
        pltpu.make_async_copy(w_q, q_whole, w_sem.at[0]),
        pltpu.make_async_copy(w_o, o_whole, w_sem.at[1]),
    ]
    for store in stores:
        store.start()
    for k in range(1, n):
        bias_copy(k).wait_recv()

    def rows_copies(b, k):
        target = lax.rem(me + k, n)
        return [
            pltpu.make_async_remote_copy(
                src_ref=src,
                dst_ref=dst,
                send_sem=rows_send.at[a, b, k],
                recv_sem=rows_recv.at[a, b, k],
                device_id={"tensor": target},
                device_id_type=MESH,
            )
            for a, (src, dst) in enumerate(
                (
                    (normed_out.at[b], normed_all.at[me, b]),
                    (att_out.at[b, :, aligned(target * share, share)], att_all.at[me, b]),
                )
            )
        ]

    def own_copies(b):
        return [
            pltpu.make_async_copy(normed_out.at[b], normed_all.at[me, b], own_sem.at[0]),
            pltpu.make_async_copy(
                att_out.at[b, :, aligned(me * share, share)], att_all.at[me, b], own_sem.at[1]
            ),
        ]

    def swap_copies(b, k):
        return [
            pltpu.make_async_remote_copy(
                src_ref=ref.at[mine, b],
                dst_ref=ref.at[mine, b],
                send_sem=swap_send.at[a, b, k],
                recv_sem=swap_recv.at[a, b, k],
                device_id={"dp": lax.rem(d + 2 * k, dp)},
                device_id_type=MESH,
            )
            for a, ref in enumerate((two_hbm, act_hbm))
        ]

    def pairs_copy(b, k):
        rows_here = aligned(b * block + me * own, own)
        return pltpu.make_async_remote_copy(
            src_ref=kv_out.at[rows_here],
            dst_ref=kv_out.at[rows_here],
            send_sem=kv_send.at[k],
            recv_sem=kv_recv.at[k],
            device_id={"tensor": lax.rem(me + k, n)},
            device_id_type=MESH,
        )

    def hand_copy(b):
        return pltpu.make_async_remote_copy(
            src_ref=result_out.at[b],
            dst_ref=inbox.at[b],
            send_sem=hand_send.at[b],
            recv_sem=hand_recv.at[b],
            device_id={"section": 1 - sec},
            device_id_type=MESH,
        )

    def keep_copies(b, c):
        return [
            pltpu.make_async_copy(g.at[c], two_hbm.at[mine, b, c], keep_sem.at[0, c]),
            pltpu.make_async_copy(act.at[c], act_hbm.at[mine, b, c], keep_sem.at[1, c]),
            pltpu.make_async_copy(slope.at[c], slope_hbm.at[b, c], keep_sem.at[2, c]),
        ]

    def block_step(b, carry):
        @pl.when(sec == 0)
        def _():
            input_out[b] = tokens[b]

        @pl.when(sec != 0)
        def _():
            hand_copy(b).wait_recv()
            input_out[b] = inbox[b]

        x_ref[...] = input_out[b].astype(F32)
        unit, _ = normalize(x_ref[...])
        normed = (unit * vecs[0:1] + vecs[1:2]).astype(BF16)
        normed_out[b] = normed
        pairs = (dot(normed, w_kv[...]) + pair_bias[...]).astype(BF16)
        kv_out[aligned(b * block + me * own, own)] = pairs
        for k in range(1, n):
            pairs_copy(b, k).start()
        for k in range(1, n):
            rows_copies(b, k)[0].start()
        own_copies(b)[0].start()

        def query_tile(t, carry):
            cols = aligned(t * q_tile, q_tile)
            bias = bias_q[t // (share // q_tile), 0:1, aligned(lax.rem(t, share // q_tile) * q_tile, q_tile)]
            q = (dot(normed_out[b], w_q[:, cols]) + bias).astype(BF16)
            for k in range(q_tile // HD):
                q_ref[aligned((t * (q_tile // HD) + k) * own, own)] = q[:, k * HD : (k + 1) * HD]
            return carry

        lax.fori_loop(0, width // q_tile, query_tile, 0)
        query_out[b] = q_ref[...]
        for k in range(1, n):
            pairs_copy(b, k).wait_recv()
        here = aligned(b * block, block)
        v_t[b] = kv_out[here, HD:].astype(F32).T.astype(BF16)

        def head_tile(t, carry):
            q = q_ref[aligned(t * per * own, per * own)]

            def score(kb, top):
                s = dot_t(kv_out[aligned(kb * block, block), :HD], q) * scale
                s_ref[kb] = s
                return jnp.maximum(top, jnp.max(s, axis=0, keepdims=True))

            top = lax.fori_loop(0, b + 1, score, jnp.full((1, per * own), -jnp.inf, F32))

            def weigh(kb, state):
                total, acc = state
                e = jnp.exp(s_ref[kb] - top)
                return total + jnp.sum(e, axis=0, keepdims=True), acc + dot(v_t[kb], e.astype(BF16))

            total, acc = lax.fori_loop(
                0,
                b + 1,
                weigh,
                (jnp.zeros((1, per * own), F32), jnp.zeros((HD, per * own), F32)),
            )
            lse_out[b, t] = top + jnp.log(total)
            mixed = (acc / total).T.astype(BF16)
            for k in range(per):
                att_out[b, :, aligned((t * per + k) * HD, HD)] = mixed[k * own : (k + 1) * own]
            return carry

        lax.fori_loop(0, heads // per, head_tile, 0)
        for k in range(1, n):
            rows_copies(b, k)[1].start()
        own_copies(b)[1].start()

        def out_tile(t, carry):
            cols = aligned(t * tile, tile)
            hidden_out[b, :, cols] = (
                x_ref[:, cols] + dot(att_out[b], w_o[:, cols]) + vecs[4:5, cols]
            )
            return carry

        lax.fori_loop(0, dim // tile, out_tile, 0)
        unit, _ = normalize(hidden_out[b])
        normed_two = (unit * vecs[2:3] + vecs[3:4]).astype(BF16)
        for c in range(chunks):
            g[c, aligned(me * rows, rows)] = normed_two[c * rows : (c + 1) * rows]

        @pl.when(b == 0)
        def _():
            loads[2].wait()
            loads[3].wait()

        def compute(c):
            def up_tile(t, carry):
                cols = aligned(t * tile, tile)
                pre = dot(g[c], w_up[:, cols]) + up_bias[:, cols]
                inner = GELU_A * (pre + GELU_B * pre * pre * pre)
                th = jnp.tanh(inner)
                half = 0.5 * (1.0 + th)
                act[c, :, cols] = (pre * half).astype(BF16)
                slope[c, :, cols] = (
                    half + 0.5 * pre * (1.0 - th * th) * (GELU_A * (1.0 + 3.0 * GELU_B * pre * pre))
                ).astype(BF16)
                return carry

            lax.fori_loop(0, ff // tile, up_tile, 0)

            def down_tile(t, carry):
                cols = aligned(t * tile, tile)
                terms[c, :, cols] = dot(act[c], w_dn[:, cols])
                return carry

            lax.fori_loop(0, dim // tile, down_tile, 0)
            for copy in keep_copies(b, c):
                copy.start()

        def finish(c, what):
            for copy in keep_copies(b, c):
                copy.wait()

        line_rounds(
            n,
            chunks,
            rows,
            {
                "refs": (g, terms, sum_r, sum_l, in_l, in_r),
                "sems": (gs_r, gs_l, g_recv, rs_r, rs_l, rr_l, rr_r),
            },
            compute,
            finish,
        )
        for c in range(chunks):
            part = slice(c * rows, (c + 1) * rows)
            result_out[b, part] = (
                hidden_out[b, part] + terms[c, aligned(me * rows, rows)] + vecs[5:6]
            ).astype(BF16)

        @pl.when(sec == 0)
        def _():
            hand_copy(b).start()

        @pl.when(b < nb - 1)
        def _():
            for k in range(1, peers):
                for copy in swap_copies(b, k):
                    copy.start()

        for k in range(1, n):
            pairs_copy(b, k).wait_send()
        for copy in own_copies(b):
            copy.wait()
        return carry

    lax.fori_loop(0, nb, block_step, 0)

    def settle(b, carry):
        @pl.when(sec == 0)
        def _():
            hand_copy(b).wait_send()

        for k in range(1, n):
            for copy in rows_copies(b, k):
                copy.wait()

        @pl.when(b < nb - 1)
        def _():
            for k in range(1, peers):
                for copy in swap_copies(b, k):
                    copy.wait()

        return carry

    lax.fori_loop(0, nb, settle, 0)
    for relay, complete, drain in gathers:
        drain()
    for k in range(1, n):
        bias_copy(k).wait_send()
    for store in stores:
        store.wait()


def forward(tokens, q_shard, o_shard, w_up, w_dn, w_kv, vecs, q_bias, up_bias, pair_bias):
    n = lax.axis_size("tensor")
    dp = lax.axis_size("dp")
    peers = dp // 2
    nb, own, dim = tokens.shape
    rows = min(16, own)
    chunks = own // rows
    ff = w_up.shape[1]
    share = q_shard.shape[1]
    width = share * n
    heads = width // HD
    tile = min(512, dim, ff)
    per = min(heads, max(1, 256 // own))
    block = n * own
    cfg = dict(n=n, nb=nb, own=own, chunks=chunks, rows=rows, tile=tile, per=per)
    S = jax.ShapeDtypeStruct
    vmem = pl.BlockSpec(memory_space=pltpu.VMEM)
    hbm = pl.BlockSpec(memory_space=pl.ANY)
    line_refs, line_sems = line_scratch(n, chunks, rows, dim)
    dma = pltpu.SemaphoreType.DMA
    return pl.pallas_call(
        functools.partial(forward_kernel, cfg),
        name="forward",
        out_shape=(
            S((nb, heads * own, HD), BF16),
            S((nb, heads // per, 1, per * own), F32),
            S((nb, own, dim), BF16),
            S((nb, own, dim), F32),
            S((nb, own, dim), BF16),
            S((nb * block, 2 * HD), BF16),
            S((peers, nb, chunks, n * rows, dim), BF16),
            S((peers, nb, chunks, n * rows, ff), BF16),
            S((nb, chunks, n * rows, ff), BF16),
            S((n, nb, own, dim), BF16),
            S((n, nb, own, share), BF16),
            S((dim, width), BF16),
            S((width, dim), BF16),
        ),
        in_specs=[vmem, hbm, hbm, hbm, hbm, vmem, vmem, vmem, vmem, vmem],
        out_specs=(vmem,) * 6 + (hbm,) * 7,
        scratch_shapes=[
            pltpu.VMEM((nb, own, dim), BF16),
            pltpu.VMEM((nb, own, width), BF16),
            pltpu.VMEM((n, 8, share), F32),
            pltpu.VMEM((dim, width), BF16),
            pltpu.VMEM((width, dim), BF16),
            pltpu.VMEM((dim, ff), BF16),
            pltpu.VMEM((ff, dim), BF16),
            pltpu.VMEM((own, dim), F32),
            pltpu.VMEM((heads * own, HD), BF16),
            pltpu.VMEM((nb, HD, block), BF16),
            pltpu.VMEM((nb, block, per * own), F32),
            pltpu.VMEM((chunks, n * rows, ff), BF16),
            pltpu.VMEM((chunks, n * rows, ff), BF16),
            pltpu.VMEM((nb, own, dim), BF16),
            *line_refs,
            *line_sems,
            dma((4,)),
            dma((n,)),
            dma((n,)),
            dma((3, chunks)),
            dma((nb,)),
            dma((nb,)),
            dma((2, n)),
            dma((2, peers, n)),
            dma((2, peers, n)),
            dma((2, n)),
            dma((2, n)),
            dma((2, peers, n)),
            dma((2, peers, n)),
            dma((2, peers, n)),
            dma((n,)),
            dma((n,)),
            dma((2, nb, n)),
            dma((2, nb, n)),
            dma((2,)),
            dma((2, nb, peers)),
            dma((2, nb, peers)),
        ],
        compiler_params=pltpu.CompilerParams(
            collective_id=1, has_side_effects=True, vmem_limit_bytes=67000000
        ),
    )(tokens, q_shard, o_shard, w_up, w_dn, w_kv, vecs, q_bias, up_bias, pair_bias)


def norm_back(v, gain, grad):
    unit, rstd = normalize(v)
    scaled = grad * gain
    mean_one = jnp.mean(scaled, axis=-1, keepdims=True)
    mean_two = jnp.mean(scaled * unit, axis=-1, keepdims=True)
    back = rstd * (scaled - mean_one - unit * mean_two)
    return back, jnp.sum(grad * unit, axis=0, keepdims=True), jnp.sum(grad, axis=0, keepdims=True)


def backward_kernel(
    cfg,
    cot,
    inputs,
    hidden,
    query,
    lse,
    kv,
    vecs,
    w_kv,
    slope_hbm,
    w_dn_hbm,
    w_up_hbm,
    w_o_hbm,
    w_q_hbm,
    two_in,
    act_in,
    input_grad,
    common,
    up_sum,
    mlp_hbm,
    pre_hbm,
    branch_all,
    gq_all,
    pairs_all,
    two_hbm,
    act_hbm,
    branch_out,
    gq_out,
    pairs_out,
    z_sum,
    dp_sum,
    w_dn,
    w_up,
    w_o,
    w_q,
    go,
    gn,
    slope,
    gpre,
    p_ref,
    g_ref,
    gk,
    gv,
    k_t,
    ga,
    inbox,
    hand,
    pair_send,
    pair_recv,
    g,
    terms,
    sum_r,
    sum_l,
    in_l,
    in_r,
    gs_r,
    gs_l,
    g_recv,
    rs_r,
    rs_l,
    rr_l,
    rr_r,
    w_sem,
    ps_sem,
    pr_sem,
    keep_sem,
    slope_sem,
    hand_send,
    hand_recv,
    rows_send,
    rows_recv,
    own_sem,
    swap_send,
    swap_recv,
    z_send,
    z_recv,
    dp_send,
    dp_recv,
):
    n, nb, own, chunks, rows, tile = (cfg[k] for k in ("n", "nb", "own", "chunks", "rows", "tile"))
    per = cfg["per"]
    dp = lax.axis_size("dp")
    d = lax.axis_index("dp")
    peers, rank = dp // 2, d // 2
    share = w_q.shape[1] // n
    dim = go.shape[1]
    ff = w_up.shape[1]
    width = w_q.shape[1]
    heads = width // HD
    block = n * own
    me = lax.axis_index("tensor")
    sec = lax.axis_index("section")
    scale = 1.0 / math.sqrt(HD)
    loads = [
        pltpu.make_async_copy(src, dst, w_sem.at[k])
        for k, (src, dst) in enumerate(((w_dn_hbm, w_dn), (w_up_hbm, w_up), (w_o_hbm, w_o), (w_q_hbm, w_q)))
    ]
    for load in loads:
        load.start()
    greet(n)

    def rows_copies(b, k):
        target = lax.rem(me + k, n)
        return [
            pltpu.make_async_remote_copy(
                src_ref=src,
                dst_ref=dst,
                send_sem=rows_send.at[a, b, k],
                recv_sem=rows_recv.at[a, b, k],
                device_id={"tensor": target},
                device_id_type=MESH,
            )
            for a, (src, dst) in enumerate(
                (
                    (branch_out.at[b], branch_all.at[me, b]),
                    (gq_out.at[b, :, aligned(target * share, share)], gq_all.at[me, b]),
                    (pairs_out.at[b], pairs_all.at[me, b]),
                )
            )
        ]

    def own_copies(b):
        return [
            pltpu.make_async_copy(branch_out.at[b], branch_all.at[me, b], own_sem.at[0]),
            pltpu.make_async_copy(
                gq_out.at[b, :, aligned(me * share, share)], gq_all.at[me, b], own_sem.at[1]
            ),
            pltpu.make_async_copy(pairs_out.at[b], pairs_all.at[me, b], own_sem.at[2]),
        ]

    def swap_copies(b, k):
        return [
            pltpu.make_async_remote_copy(
                src_ref=ref.at[rank, b],
                dst_ref=ref.at[rank, b],
                send_sem=swap_send.at[a, b, k],
                recv_sem=swap_recv.at[a, b, k],
                device_id={"dp": lax.rem(d + 2 * k, dp)},
                device_id_type=MESH,
            )
            for a, ref in enumerate((mlp_hbm, pre_hbm))
        ]

    def late_copies(k):
        return [
            pltpu.make_async_remote_copy(
                src_ref=ref.at[rank, nb - 1],
                dst_ref=ref.at[rank, nb - 1],
                send_sem=swap_send.at[2 + a, 0, k],
                recv_sem=swap_recv.at[2 + a, 0, k],
                device_id={"dp": lax.rem(d + 2 * k, dp)},
                device_id_type=MESH,
            )
            for a, ref in enumerate((two_hbm, act_hbm))
        ]

    for k in range(1, peers):
        for copy in late_copies(k):
            copy.start()
    gk[...] = jnp.zeros_like(gk)
    gv[...] = jnp.zeros_like(gv)
    common[...] = jnp.zeros_like(common)
    up_sum[...] = jnp.zeros_like(up_sum)
    for kb in range(nb):
        k_t[kb] = kv[kb * block : (kb + 1) * block, :HD].astype(F32).T.astype(BF16)

    def pair_copy(k):
        target = lax.rem(me + k, n)
        return pltpu.make_async_remote_copy(
            src_ref=pair_send.at[aligned(target * own, own)],
            dst_ref=pair_recv.at[k],
            send_sem=ps_sem.at[k],
            recv_sem=pr_sem.at[k],
            device_id={"tensor": target},
            device_id_type=MESH,
        )

    def hand_copy(b):
        return pltpu.make_async_remote_copy(
            src_ref=hand,
            dst_ref=inbox.at[b],
            send_sem=hand_send,
            recv_sem=hand_recv.at[b],
            device_id={"section": 1 - sec},
            device_id_type=MESH,
        )

    def keep_copies(b, c):
        return [
            pltpu.make_async_copy(g.at[c], mlp_hbm.at[rank, b, c], keep_sem.at[0, c]),
            pltpu.make_async_copy(gpre.at[c], pre_hbm.at[rank, b, c], keep_sem.at[1, c]),
        ]

    def block_step(i, carry):
        b = nb - 1 - i
        slope_load = pltpu.make_async_copy(slope_hbm.at[b], slope, slope_sem)
        slope_load.start()

        @pl.when(sec == 1)
        def _():
            go[...] = cot[b].astype(F32)

        @pl.when(sec != 1)
        def _():
            hand_copy(b).wait_recv()
            go[...] = inbox[b].astype(F32)

        common[5:6, :dim] += jnp.sum(go[...], axis=0, keepdims=True)
        for c in range(chunks):
            g[c, aligned(me * rows, rows)] = go[c * rows : (c + 1) * rows].astype(BF16)
        slope_load.wait()

        @pl.when(i == 0)
        def _():
            loads[0].wait()
            loads[1].wait()

        def compute(c):
            def act_tile(t, carry):
                cols = aligned(t * tile, tile)
                grad = (dot_t(g[c], w_dn[cols]) * slope[c, :, cols].astype(F32)).astype(BF16)
                gpre[c, :, cols] = grad
                up_sum[:, cols] += jnp.sum(grad.astype(F32), axis=0, keepdims=True)
                return carry

            lax.fori_loop(0, ff // tile, act_tile, 0)

            def back_tile(t, carry):
                cols = aligned(t * tile, tile)
                terms[c, :, cols] = dot_t(gpre[c], w_up[cols])
                return carry

            lax.fori_loop(0, dim // tile, back_tile, 0)
            for copy in keep_copies(b, c):
                copy.start()

        def finish(c, what):
            for copy in keep_copies(b, c):
                copy.wait()

        line_rounds(
            n,
            chunks,
            rows,
            {
                "refs": (g, terms, sum_r, sum_l, in_l, in_r),
                "sems": (gs_r, gs_l, g_recv, rs_r, rs_l, rr_l, rr_r),
            },
            compute,
            finish,
        )
        for k in range(1, peers):
            for copy in swap_copies(b, k):
                copy.start()
        for c in range(chunks):
            gn[c * rows : (c + 1) * rows] = terms[c, aligned(me * rows, rows)]
        back, gain_sum, bias_sum = norm_back(hidden[b], vecs[2:3], gn[...])
        common[3:4, :dim] += gain_sum
        common[4:5, :dim] += bias_sum
        go[...] += back
        common[2:3, :dim] += jnp.sum(go[...], axis=0, keepdims=True)
        branch_out[b] = go[...].astype(BF16)
        for k in range(1, n):
            rows_copies(b, k)[0].start()
        own_copies(b)[0].start()

        @pl.when(i == 0)
        def _():
            loads[2].wait()

        def att_tile(t, carry):
            grad = dot_t(branch_out[b], w_o[aligned(t * tile, tile)]).astype(BF16)
            for k in range(tile // HD):
                ga[aligned((t * (tile // HD) + k) * own, own)] = grad[:, k * HD : (k + 1) * HD]
            return carry

        lax.fori_loop(0, width // tile, att_tile, 0)

        def head_tile(t, carry):
            here = aligned(t * per * own, per * own)
            q = query[b, here]
            grad = ga[here]
            log_total = lse[b, t]

            def first(kb, inner):
                keys = aligned(kb * block, block)
                prob = jnp.exp(dot_t(kv[keys, :HD], q) * scale - log_total)
                grad_prob = dot_t(kv[keys, HD:], grad)
                p_ref[kb] = prob
                g_ref[kb] = grad_prob
                return inner + jnp.sum(prob * grad_prob, axis=0, keepdims=True)

            inner = lax.fori_loop(0, b + 1, first, jnp.zeros((1, per * own), F32))

            def second(kb, acc):
                keys = aligned(kb * block, block)
                prob = p_ref[kb]
                grad_score = (prob * (g_ref[kb] - inner)).astype(BF16)
                gk[keys] += dot(grad_score, q)
                gv[keys] += dot(prob.astype(BF16), grad)
                return acc + dot(k_t[kb], grad_score)

            acc = lax.fori_loop(0, b + 1, second, jnp.zeros((HD, per * own), F32))
            back = (acc * scale).T.astype(BF16)
            for k in range(per):
                gq_out[b, :, aligned((t * per + k) * HD, HD)] = back[k * own : (k + 1) * own]
            return carry

        lax.fori_loop(0, heads // per, head_tile, 0)
        here = aligned(b * block, block)
        pair_send[:, :HD] = (gk[here] * scale).astype(BF16)
        pair_send[:, HD:] = gv[here].astype(BF16)
        for k in range(1, n):
            pair_copy(k).start()
        for k in range(1, n):
            rows_copies(b, k)[1].start()
        own_copies(b)[1].start()
        common[6:7, :width] += jnp.sum(gq_out[b].astype(F32), axis=0, keepdims=True)

        @pl.when(i == 0)
        def _():
            loads[3].wait()

        def normed_tile(t, carry):
            cols = aligned(t * tile, tile)
            gn[:, cols] = dot_t(gq_out[b], w_q[cols])
            return carry

        lax.fori_loop(0, dim // tile, normed_tile, 0)
        mine = aligned(b * block + me * own, own)
        total_k = gk[mine] * scale
        total_v = gv[mine]
        for k in range(1, n):
            pair_copy(k).wait_recv()
            total_k += pair_recv[k, :, :HD].astype(F32)
            total_v += pair_recv[k, :, HD:].astype(F32)
        pairs_out[b, :, :HD] = total_k.astype(BF16)
        pairs_out[b, :, HD:] = total_v.astype(BF16)
        for k in range(1, n):
            rows_copies(b, k)[2].start()
        own_copies(b)[2].start()
        common[7:8, : 2 * HD] += jnp.sum(pairs_out[b].astype(F32), axis=0, keepdims=True)

        def pair_tile(t, carry):
            cols = aligned(t * tile, tile)
            gn[:, cols] += dot_t(pairs_out[b], w_kv[cols])
            return carry

        lax.fori_loop(0, dim // tile, pair_tile, 0)
        back, gain_sum, bias_sum = norm_back(inputs[b].astype(F32), vecs[0:1], gn[...])
        common[0:1, :dim] += gain_sum
        common[1:2, :dim] += bias_sum
        go[...] += back
        input_grad[b] = go[...]
        for k in range(1, n):
            pair_copy(k).wait_send()

        @pl.when(sec == 1)
        def _():
            @pl.when(i > 0)
            def _():
                hand_copy(b).wait_send()

            hand[...] = go[...].astype(BF16)
            hand_copy(b).start()

        for copy in own_copies(b):
            copy.wait()
        return carry

    lax.fori_loop(0, nb, block_step, 0)

    def z_copy(k):
        return pltpu.make_async_remote_copy(
            src_ref=common,
            dst_ref=z_sum.at[me],
            send_sem=z_send.at[k],
            recv_sem=z_recv.at[k],
            device_id={"tensor": lax.rem(me + k, n)},
            device_id_type=MESH,
        )

    def dp_copy(k):
        return pltpu.make_async_remote_copy(
            src_ref=dp_sum.at[d],
            dst_ref=dp_sum.at[d],
            send_sem=dp_send.at[k],
            recv_sem=dp_recv.at[k],
            device_id={"dp": lax.rem(d + k, dp)},
            device_id_type=MESH,
        )

    z_sum[me] = common[...]
    for k in range(1, n):
        z_copy(k).start()
    for k in range(1, n):
        z_copy(k).wait()
    total = z_sum[0]
    for j in range(1, n):
        total += z_sum[j]
    dp_sum[d, :8] = total
    dp_sum[d, 8:] = jnp.zeros((8, total.shape[1]), F32)
    dp_sum[d, 8:9, :ff] = up_sum[...]
    for k in range(1, dp):
        dp_copy(k).start()
    for k in range(1, dp):
        dp_copy(k).wait()
    total = dp_sum[0]
    for j in range(1, dp):
        total += dp_sum[j]
    common[...] = total[:8]
    up_sum[...] = total[8:9, :ff]

    def settle(b, carry):
        for k in range(1, n):
            for copy in rows_copies(b, k):
                copy.wait()
        for k in range(1, peers):
            for copy in swap_copies(b, k):
                copy.wait()
        return carry

    lax.fori_loop(0, nb, settle, 0)
    for k in range(1, peers):
        for copy in late_copies(k):
            copy.wait()

    @pl.when(sec == 1)
    def _():
        hand_copy(0).wait_send()


def backward(cot, inputs, hidden, query, lse, kv, vecs, w_kv, slope, w_dn, w_up, w_o, w_q, two, act):
    n = lax.axis_size("tensor")
    dp = lax.axis_size("dp")
    peers = dp // 2
    nb, own, dim = cot.shape
    chunks, rows = slope.shape[1], own // slope.shape[1]
    ff = w_up.shape[1]
    width = w_q.shape[1]
    heads = width // HD
    tile = min(512, dim, ff)
    per = lse.shape[3] // own
    block = n * own
    span = max(dim, width)
    assert ff <= span
    cfg = dict(n=n, nb=nb, own=own, chunks=chunks, rows=rows, tile=tile, per=per)
    S = jax.ShapeDtypeStruct
    vmem = pl.BlockSpec(memory_space=pltpu.VMEM)
    hbm = pl.BlockSpec(memory_space=pl.ANY)
    line_refs, line_sems = line_scratch(n, chunks, rows, dim)
    dma = pltpu.SemaphoreType.DMA
    return pl.pallas_call(
        functools.partial(backward_kernel, cfg),
        name="backward",
        out_shape=(
            S((nb, own, dim), F32),
            S((8, span), F32),
            S((1, ff), F32),
            S((peers, nb, chunks, n * rows, dim), BF16),
            S((peers, nb, chunks, n * rows, ff), BF16),
            S((n, nb, own, dim), BF16),
            S((n, nb, own, width // n), BF16),
            S((n, nb, own, 2 * HD), BF16),
            S(two.shape, BF16),
            S(act.shape, BF16),
        ),
        in_specs=[vmem] * 8 + [hbm] * 7,
        out_specs=(vmem,) * 3 + (hbm,) * 7,
        input_output_aliases={13: 8, 14: 9},
        scratch_shapes=[
            pltpu.VMEM((nb, own, dim), BF16),
            pltpu.VMEM((nb, own, width), BF16),
            pltpu.VMEM((nb, own, 2 * HD), BF16),
            pltpu.VMEM((n, 8, span), F32),
            pltpu.VMEM((dp, 16, span), F32),
            pltpu.VMEM((ff, dim), BF16),
            pltpu.VMEM((dim, ff), BF16),
            pltpu.VMEM((width, dim), BF16),
            pltpu.VMEM((dim, width), BF16),
            pltpu.VMEM((own, dim), F32),
            pltpu.VMEM((own, dim), F32),
            pltpu.VMEM((chunks, n * rows, ff), BF16),
            pltpu.VMEM((chunks, n * rows, ff), BF16),
            pltpu.VMEM((nb, block, per * own), F32),
            pltpu.VMEM((nb, block, per * own), F32),
            pltpu.VMEM((nb * block, HD), F32),
            pltpu.VMEM((nb * block, HD), F32),
            pltpu.VMEM((nb, HD, block), BF16),
            pltpu.VMEM((heads * own, HD), BF16),
            pltpu.VMEM((nb, own, dim), BF16),
            pltpu.VMEM((own, dim), BF16),
            pltpu.VMEM((block, 2 * HD), BF16),
            pltpu.VMEM((n, own, 2 * HD), BF16),
            *line_refs,
            *line_sems,
            dma((4,)),
            dma((n,)),
            dma((n,)),
            dma((2, chunks)),
            dma(()),
            dma(()),
            dma((nb,)),
            dma((3, nb, n)),
            dma((3, nb, n)),
            dma((3,)),
            dma((4, nb, peers)),
            dma((4, nb, peers)),
            dma((n,)),
            dma((n,)),
            dma((dp,)),
            dma((dp,)),
        ],
        compiler_params=pltpu.CompilerParams(
            collective_id=2, has_side_effects=True, vmem_limit_bytes=67000000
        ),
    )(cot, inputs, hidden, query, lse, kv, vecs, w_kv, slope, w_dn, w_up, w_o, w_q, two, act)


def t_dot(a, b):
    return lax.dot_general(a, b, (((0,), (0,)), ((), ())), preferred_element_type=F32)


def swap(value, distance):
    size = lax.axis_size("dp")
    return lax.ppermute(value, "dp", [(i, i ^ distance) for i in range(size)])


def fold(value, distance, axis):
    bit = (lax.axis_index("dp") // distance) % 2
    half = value.shape[axis] // 2
    away = lax.dynamic_slice_in_dim(value, (1 - bit) * half, half, axis)
    kept = lax.dynamic_slice_in_dim(value, bit * half, half, axis)
    return kept + swap(away.astype(BF16), distance).astype(F32)


def unfold(value, distance, axis):
    bit = (lax.axis_index("dp") // distance) % 2
    other = swap(value, distance)
    low = jnp.where(bit == 0, value, other)
    high = jnp.where(bit == 0, other, value)
    return jnp.concatenate([low, high], axis=axis)


def sum_dp(value, axis):
    size = lax.axis_size("dp")
    distance = 1
    while distance < size:
        value = fold(value, distance, axis)
        distance *= 2
    value = value.astype(BF16)
    while distance > 1:
        distance //= 2
        value = unfold(value, distance, axis)
    return value.astype(F32)


def sum_pair(value):
    value = value.astype(BF16)
    return value.astype(F32) + swap(value, 1).astype(F32)


def on_device(
    tokens_in,
    cotangent,
    ln1_gain,
    ln1_bias,
    q_weight,
    q_bias,
    kv_weight,
    v_bias,
    o_weight,
    o_bias,
    ln2_gain,
    ln2_bias,
    up_weight,
    up_bias,
    down_weight,
    down_bias,
):
    tensor_count = lax.axis_size("tensor")
    tensor_rank = lax.axis_index("tensor")
    gain_one = ln1_gain[0].astype(F32)
    bias_one = ln1_bias[0].astype(F32)
    w_pairs = kv_weight[0]
    pair_bias = jnp.concatenate([jnp.zeros((HD,), F32), v_bias[0].astype(F32)])
    b_out = o_bias[0].astype(F32)
    gain_two = ln2_gain[0].astype(F32)
    bias_two = ln2_bias[0].astype(F32)
    w_up = up_weight[0]
    b_up = up_bias[0].astype(F32)
    w_down = down_weight[0]
    b_down = down_bias[0].astype(F32)
    blocks, own_count, seq_count, model_dim = tokens_in.shape
    assert seq_count == 1
    tokens_in = tokens_in[:, :, 0]
    cotangent = cotangent[:, :, 0]
    share = q_weight.shape[2]
    width = share * tensor_count
    query_bias = jnp.broadcast_to(q_bias.astype(F32), (8, share))

    vecs = jnp.stack([gain_one, bias_one, gain_two, bias_two, b_out, b_down, b_down, b_down])
    (
        kept_query,
        kept_logsum,
        kept_input,
        kept_hidden,
        outputs,
        kv_cache,
        normed_two,
        active,
        slope,
        normed_all,
        att_all,
        w_query,
        w_out,
    ) = forward(
        tokens_in,
        q_weight[0],
        o_weight[0],
        w_up,
        w_down,
        w_pairs,
        vecs,
        query_bias,
        b_up[None],
        pair_bias[None],
    )
    (
        input_grads,
        common,
        up_b,
        grad_mlp,
        grad_pre,
        branch_all,
        gq_all,
        pairs_all,
        normed_two,
        active,
    ) = backward(
        cotangent,
        kept_input,
        kept_hidden,
        kept_query,
        kept_logsum,
        kv_cache,
        vecs,
        w_pairs,
        slope,
        w_down,
        w_up,
        w_out,
        w_query,
        normed_two,
        active,
    )

    def flat(kept):
        return kept.reshape(-1, kept.shape[-1])

    query_w = sum_dp(t_dot(flat(normed_all), flat(gq_all)), 0)
    out_w = sum_dp(t_dot(flat(att_all), flat(branch_all)), 1)
    pair_w = sum_dp(t_dot(flat(normed_all), flat(pairs_all)), 0)
    down_w = sum_pair(t_dot(flat(active), flat(grad_mlp)))
    up_w = sum_pair(t_dot(flat(normed_two), flat(grad_pre)))
    own_query = lax.dynamic_slice_in_dim(common[6, :width], tensor_rank * share, share, 0)
    value_b = common[7, HD : 2 * HD]
    vecs = common[:6, :model_dim]
    return (
        outputs[None, :, :, None],
        input_grads[None, :, :, None],
        vecs[0][None],
        vecs[1][None],
        query_w[None],
        own_query[None],
        pair_w[None],
        value_b[None],
        out_w[None],
        vecs[2][None],
        vecs[3][None],
        vecs[4][None],
        up_w[None],
        up_b,
        down_w[None],
        vecs[5][None],
    )


def solution(mesh):
    placed = (
        P(None, "tensor", "dp", None),
        P(None, "tensor", "dp", None),
        P("section", None),
        P("section", None),
        P("section", None, "tensor"),
        P("section", "tensor"),
        P("section", None, None),
        P("section", None),
        P("section", "tensor", None),
        P("section", None),
        P("section", None),
        P("section", None),
        P("section", None, "tensor"),
        P("section", "tensor"),
        P("section", "tensor", None),
        P("section", None),
    )
    return jax.shard_map(
        on_device,
        mesh=mesh,
        in_specs=placed,
        out_specs=(
            P("section", None, "tensor", "dp", None),
            P("section", None, "tensor", "dp", None),
            P("section", None),
            P("section", None),
            P("section", None, "tensor"),
            P("section", "tensor"),
            P("section", None, None),
            P("section", None),
            P("section", "tensor", None),
            P("section", None),
            P("section", None),
            P("section", None),
            P("section", None, "tensor"),
            P("section", "tensor"),
            P("section", "tensor", None),
            P("section", None),
        ),
        check_vma=False,
    )
```
